512 devices in a mesh: subj: 8 (over z), vox: 64 (over y, x, core).
Axes of the slice: x: 4, y: 8, z: 8, core: 2. Of those that a mesh axis runs over, the one named last changes fastest.
Arguments:
- data: bfloat16 [8, 450, 65536], P('subj', None, 'vox'), may hold values from -6 to 6
- maps: bfloat16 [8, 256, 65536], P('subj', None, 'vox'), may hold values from -0.0234375 to 0.0234375
Outputs:
- response: float32 [450, 256], replicated
- new_maps: bfloat16 [8, 256, 65536], P('subj', None, 'vox')
The draws below stay inside these ranges and needn't reach their ends.
All inputs are finite; a program needn't handle non-finite values.
Results may differ from the reference program's by a relative error of at most 0.0043.
The reference program's roundings to bfloat16 on the way count: a program that leaves them out, or rounds other values in their place, can miss the bound.
Values sent between devices are 32-bit elements; how exact they have to be, the bound alone decides.
A program may use at most 64 MiB of HBM per device.

```python
import jax
import jax.numpy as jnp
from jax import lax

K = 256
TRS = 450
ITERS = 1
NS_STEPS = 5
SUBJECTS = 8
GRAYORDINATE_NUM = 65536


def block_levels(stream_key, shape, pieces, least, high):
    factor_of, own = 1.0, jax.random.fold_in(stream_key, 6)
    for dim, blocks in pieces:
        heights = jnp.exp(jax.random.uniform(jax.random.fold_in(own, dim), (blocks,), jnp.float32, least / len(pieces), high / len(pieces)))
        factor_of = factor_of * jnp.repeat(heights, shape[dim] // blocks).reshape([-1 if axis == dim else 1 for axis in range(len(shape))])
    return factor_of


def gaussian(stream_key, dims, deviation, reach, pieces=(), kind=jnp.bfloat16):
    drawn = jax.random.normal(stream_key, dims, jnp.float32) * deviation
    if len(pieces) > 0:
        drawn = block_levels(stream_key, dims, pieces, -0.22, 0.18) * drawn
    return jnp.clip(drawn, min=-reach, max=reach).astype(kind)


def setup_inputs(seed: int = 0) -> dict:
    streams_of = jax.random.split(jax.random.key(seed), 3)
    return {
        "data": gaussian(streams_of[0], (SUBJECTS, TRS, GRAYORDINATE_NUM), 1.0, 6.0, ((0, 8), (2, 64))),
        "maps": gaussian(streams_of[1], (SUBJECTS, K, GRAYORDINATE_NUM), GRAYORDINATE_NUM ** -0.5, 0.0234375, ((0, 8), (2, 64))),
    }


def whiten(gram):
    scale = jnp.sqrt(jnp.sum(gram * gram) + 1e-06)
    present_estimate = gram / scale
    eye = jnp.eye(gram.shape[0], dtype=jnp.float32)
    inverse = eye
    for step in range(NS_STEPS):
        middle = 1.5 * eye - 0.5 * jnp.dot(inverse, present_estimate, precision=lax.Precision.HIGHEST)
        present_estimate = jnp.dot(present_estimate, middle, precision=lax.Precision.HIGHEST)
        inverse = jnp.dot(middle, inverse, precision=lax.Precision.HIGHEST)
    return inverse / jnp.sqrt(scale)

def reference(data, maps):
    present_estimate = [maps[i] for i in range(SUBJECTS)]
    response = jnp.zeros((TRS, K), jnp.float32)
    for it in range(ITERS):
        total = jnp.zeros((TRS, K), jnp.float32)
        for i in range(SUBJECTS):
            total = total + jnp.dot(data[i], present_estimate[i].T, preferred_element_type=jnp.float32)
        response = total / SUBJECTS
        common_signal = response.astype(jnp.bfloat16)
        for i in range(SUBJECTS):
            projected_signal = jnp.dot(common_signal.T, data[i], preferred_element_type=jnp.float32)
            gram = jnp.dot(projected_signal, projected_signal.T, precision=lax.Precision.HIGHEST)
            subject_factor = whiten(gram)
            present_estimate[i] = jnp.dot(subject_factor, projected_signal, precision=lax.Precision.HIGHEST).astype(jnp.bfloat16)
    return (response, jnp.stack(present_estimate))
```

```python
import functools

import jax
import jax.numpy as jnp
from jax import lax
from jax.experimental import pallas as pl
from jax.experimental.pallas import tpu as pltpu
from jax.sharding import Mesh
from jax.sharding import PartitionSpec as P

NS_STEPS = 5
LANES = 128
ROWS = 512
HALF = ROWS // 2
MESH = pl.DeviceIdType.MESH
F32, BF16 = jnp.float32, jnp.bfloat16


def dot(a, b):
    return jnp.dot(a, b, preferred_element_type=F32)


def dot_nt(a, b):
    return lax.dot_general(a, b, (((1,), (1,)), ((), ())), preferred_element_type=F32)


def split(a):
    high = a.astype(BF16)
    return high, (a - high.astype(F32)).astype(BF16)


def dot3(a, b):
    ah, al = a
    bh, bl = b
    return dot(ah, bh) + (dot(ah, bl) + dot(al, bh))


def kernel(
    sizes,
    subjects,
    data_hbm,
    maps_hbm,
    resp_hbm,
    new_hbm,
    d,
    end,
    w,
    part_r,
    part_c,
    pair_r,
    pair_c,
    sum_r,
    sum_c,
    r1,
    c1,
    r2,
    c2,
    r2_sum,
    c2_sum,
    swap,
    full_r,
    full_c,
    gram_hi,
    gram_lo,
    a_hi,
    a_lo,
    resp,
    new,
    local_sem,
    send_sem,
    recv_sem,
):
    nz, ny, nx = sizes
    trs = data_hbm.shape[1]
    me = {name: lax.axis_index(name) for name in ("subj", "y", "x", "core")}
    size = {"subj": nz, "y": ny, "x": nx, "core": 2}
    core = me["core"]
    other = 1 - core

    edge = trs // 16 * 16
    load_d = pltpu.make_async_copy(
        data_hbm.at[0, pl.ds(0, edge)], d.at[pl.ds(0, edge)], local_sem.at[0]
    )
    load_end = pltpu.make_async_copy(
        data_hbm.at[0, pl.ds(edge, trs - edge)], end, local_sem.at[2]
    )
    load_end.start()
    load_w = pltpu.make_async_copy(maps_hbm.at[0], w, local_sem.at[1])
    load_d.start()
    load_w.start()

    barrier = pltpu.get_barrier_semaphore()
    partners = 0
    for axis, n in size.items():
        for s in range(1, n):
            pl.semaphore_signal(
                barrier,
                inc=1,
                device_id={axis: lax.rem(me[axis] + s, n)},
                device_id_type=MESH,
            )
            partners += 1

    pending = []

    def send(src, dst, axis, s, arrived):
        k = len(pending)
        copy = pltpu.make_async_remote_copy(
            src_ref=src,
            dst_ref=dst,
            send_sem=send_sem.at[k],
            recv_sem=recv_sem.at[k],
            device_id={axis: lax.rem(me[axis] + s, size[axis])},
            device_id_type=MESH,
        )
        copy.start()
        pending.append(copy)
        back = pltpu.make_async_remote_copy(
            src_ref=src,
            dst_ref=arrived,
            send_sem=send_sem.at[k],
            recv_sem=recv_sem.at[k],
            device_id={axis: lax.rem(me[axis] + s, size[axis])},
            device_id_type=MESH,
        )
        return back.wait_recv

    def near_first(n):
        return sorted(range(1, n), key=lambda s: min(s, n - s))

    def far_first(n):
        return near_first(n)[::-1]

    def ahead(axis, s):
        return lax.rem(me[axis] + s, size[axis])

    def behind(axis, s):
        return lax.rem(me[axis] + (size[axis] - s), size[axis])

    def rows(start, count):
        return pl.ds(pl.multiple_of(start, 8), count)

    zeros = jnp.zeros((LANES, LANES), F32)
    for slot in range(4):
        part_c[1, pl.ds(slot * LANES, LANES)] = zeros
    load_end.wait()
    d[pl.ds(edge, ROWS - edge), :] = jnp.concatenate(
        [end[...], jnp.zeros((ROWS - trs, d.shape[1]), BF16)], axis=0
    )
    load_d.wait()
    load_w.wait()
    partial = dot_nt(d[...], w[...])
    part_r[0] = partial[:, :LANES]
    part_r[1] = partial[:, LANES:]
    pl.semaphore_wait(barrier, partners)
    got_pair_r = send(part_r.at[other], pair_r, "core", 1, pair_r)

    row = lax.broadcasted_iota(jnp.int32, (LANES, LANES), 0)
    col = lax.broadcasted_iota(jnp.int32, (LANES, LANES), 1)
    top = dot_nt(d[pl.ds(0, HALF), :], d[pl.ds(0, HALF), :])
    c00, c10, c11 = top[:LANES, :LANES], top[LANES:, :LANES], top[LANES:, LANES:]
    part_c[0, pl.ds(0, LANES)] = c10
    part_c[0, pl.ds(3 * LANES, LANES)] = jnp.where(row >= col, c00, c11)
    low = dot_nt(d[pl.ds(HALF, HALF), :], d[...])
    part_c[0, pl.ds(LANES, LANES)] = low[:LANES, :LANES]
    part_c[0, pl.ds(2 * LANES, LANES)] = low[:LANES, LANES : 2 * LANES]
    c22 = low[:LANES, 2 * LANES : 3 * LANES]
    c33 = low[LANES:, 3 * LANES :]
    last = 72
    for slot in range(3):
        part_c[1, pl.ds(slot * LANES, last)] = low[
            LANES : LANES + last, slot * LANES : (slot + 1) * LANES
        ]
    part_c[1, pl.ds(3 * LANES, LANES)] = jnp.where(row >= col, c22, c33)
    on_diagonal = row == col
    for slot, block in ((0, c11), (1, c33)):
        diagonal = jnp.sum(jnp.where(on_diagonal, block, 0.0), axis=0, keepdims=True)
        part_c[1, pl.ds(slot * LANES + 80, 8)] = jnp.broadcast_to(diagonal, (8, LANES))
    got_pair_c = send(part_c.at[other], pair_c, "core", 1, pair_c)

    lanes_of = (("subj", "y", 0), ("y", "subj", 1))
    got_pair_r()
    sum_r[...] = part_r[core] + pair_r[...]
    got = {}
    for axis, _, half in lanes_of:
        n = size[axis]
        block = HALF // n
        for s in far_first(n):
            got[half, s] = send(
                sum_r.at[rows(half * HALF + ahead(axis, s) * block, block)],
                r1.at[half, s - 1, pl.ds(0, block)],
                axis,
                s,
                r1.at[half, s - 1, pl.ds(0, block)],
            )
    got_pair_c()
    sum_c[...] = part_c[core] + pair_c[...]
    block_x = ROWS // nx
    for s in far_first(nx):
        got["c", s] = send(
            sum_c.at[rows(ahead("x", s) * block_x, block_x)], c1.at[s - 1], "x", s, c1.at[s - 1]
        )
    for axis, _, half in lanes_of:
        n = size[axis]
        block = HALF // n
        fine = block // nx
        total = sum_r[rows(half * HALF + me[axis] * block, block)]
        for s in near_first(n):
            got[half, s]()
            total = total + r1[half, s - 1, pl.ds(0, block)]
        r2_sum[half, pl.ds(0, block)] = total
        for s in far_first(nx):
            got[half, "x", s] = send(
                r2_sum.at[half, rows(ahead("x", s) * fine, fine)],
                r2.at[half, s - 1, pl.ds(0, fine)],
                "x",
                s,
                r2.at[half, s - 1, pl.ds(0, fine)],
            )
    total = sum_c[rows(me["x"] * block_x, block_x)]
    for s in near_first(nx):
        got["c", s]()
        total = total + c1[s - 1]
    c2_sum[...] = total
    fine_c = block_x // ny
    for s in far_first(ny):
        got["c", "y", s] = send(
            c2_sum.at[rows(ahead("y", s) * fine_c, fine_c)], c2.at[s - 1], "y", s, c2.at[s - 1]
        )
    for axis, across, half in lanes_of:
        fine = HALF // size[axis] // nx
        n = size[across]
        total = r2_sum[half, rows(me["x"] * fine, fine)]
        for s in near_first(nx):
            got[half, "x", s]()
            total = total + r2[half, s - 1, pl.ds(0, fine)]
        swap[half, me[across], pl.ds(0, fine)] = total
        for s in far_first(n):
            got[half, "swap", s] = send(
                swap.at[half, me[across], pl.ds(0, fine)],
                swap.at[half, me[across], pl.ds(0, fine)],
                across,
                s,
                swap.at[half, behind(across, s), pl.ds(0, fine)],
            )
    total = c2_sum[rows(me["y"] * fine_c, fine_c)]
    for s in near_first(ny):
        got["c", "y", s]()
        total = total + c2[s - 1]

    def gram_rows(x, y):
        return rows(x * block_x + y * fine_c, fine_c)

    mine = full_c.at[core, gram_rows(me["x"], me["y"])]
    mine[...] = total
    for s in far_first(ny):
        got["c", "ay", s] = send(
            mine, mine, "y", s, full_c.at[core, gram_rows(me["x"], behind("y", s))]
        )
    for axis, across, half in lanes_of:
        block = HALF // size[axis]
        fine = block // nx
        n = size[across]
        for s in near_first(n):
            got[half, "swap", s]()
        total = swap[half, 0, pl.ds(0, fine)]
        for i in range(1, n):
            total = total + swap[half, i, pl.ds(0, fine)]
        start = half * HALF + me[axis] * block
        mine = full_r.at[core, rows(start + me["x"] * fine, fine)]
        mine[...] = total * (1.0 / subjects)
        for s in far_first(nx):
            got[half, "ax", s] = send(
                mine, mine, "x", s, full_r.at[core, rows(start + behind("x", s) * fine, fine)]
            )
    for s in near_first(ny):
        got["c", "ay", s]()
    got_other = []
    mine = full_c.at[core, rows(me["x"] * block_x, block_x)]
    for s in far_first(nx):
        got["c", "ax", s] = send(
            mine, mine, "x", s, full_c.at[core, rows(behind("x", s) * block_x, block_x)]
        )
    got_other_c = [
        send(mine, mine, "core", 1, full_c.at[other, rows(me["x"] * block_x, block_x)])
    ]
    got_other_r = []
    for axis, _, half in lanes_of:
        n = size[axis]
        block = HALF // n
        for s in near_first(nx):
            got[half, "ax", s]()
        here = rows(half * HALF + me[axis] * block, block)
        mine = full_r.at[core, here]
        for s in far_first(n):
            there = rows(half * HALF + behind(axis, s) * block, block)
            got[half, "az", s] = send(mine, mine, axis, s, full_r.at[core, there])
        got_other_r.append(send(mine, mine, "core", 1, full_r.at[other, here]))
    for s in near_first(nx):
        got["c", "ax", s]()
        here = rows(behind("x", s) * block_x, block_x)
        mine = full_c.at[core, here]
        got_other_c.append(send(mine, mine, "core", 1, full_c.at[other, here]))

    def forward(hops):
        for axis, _, half in lanes_of:
            n = size[axis]
            block = HALF // n
            for s in near_first(n):
                if (min(s, n - s) <= 2) != hops:
                    continue
                got[half, "az", s]()
                here = rows(half * HALF + behind(axis, s) * block, block)
                mine = full_r.at[core, here]
                got_other_r.append(send(mine, mine, "core", 1, full_r.at[other, here]))

    forward(True)
    for wait in got_other_c:
        wait()

    def put(i, j, block):
        high, low_part = split(block)
        gram_hi[pl.ds(i * LANES, LANES), pl.ds(j * LANES, LANES)] = high
        gram_lo[pl.ds(i * LANES, LANES), pl.ds(j * LANES, LANES)] = low_part

    def put_both(i, j, block):
        put(i, j, block)
        put(j, i, block.T)

    put_both(1, 0, full_c[0, pl.ds(0, LANES)])
    put_both(2, 0, full_c[0, pl.ds(LANES, LANES)])
    put_both(2, 1, full_c[0, pl.ds(2 * LANES, LANES)])
    for slot in range(3):
        block = full_c[1, pl.ds(slot * LANES, LANES)]
        put_both(3, slot, jnp.where(row < last, block, 0.0))
    for half, i, j in ((0, 0, 1), (1, 2, 3)):
        packed = full_c[half, pl.ds(3 * LANES, LANES)]
        turned = packed.T
        diagonal = full_c[1, pl.ds(half * LANES + 80, 8)][:1]
        put(i, i, jnp.where(row >= col, packed, turned))
        block = jnp.where(row < col, packed, turned)
        put(j, j, jnp.where(on_diagonal, jnp.broadcast_to(diagonal, block.shape), block))

    forward(False)
    for wait in got_other_r:
        wait()

    response = jnp.concatenate([full_r[0], full_r[1]], axis=1)
    resp[...] = response[:trs]
    store_r = pltpu.make_async_copy(resp, resp_hbm, local_sem.at[0])
    store_r.start()
    shared = response.astype(BF16)
    shared_t = shared.T
    t = dot(shared_t, gram_hi[...]) + dot(shared_t, gram_lo[...])
    t_hi, t_lo = split(t)
    gram = dot(t_hi, shared) + dot(t_lo, shared)
    k = gram.shape[0]

    scale = jnp.sqrt(jnp.sum(gram * gram, keepdims=True) + 1e-06)
    estimate = gram / scale
    unit = lax.broadcasted_iota(jnp.int32, (k, k), 0) == lax.broadcasted_iota(
        jnp.int32, (k, k), 1
    )
    eye = jnp.where(unit, 1.5, 0.0).astype(F32)
    middle = split(eye - 0.5 * estimate)
    inverse = middle
    estimate = split(dot3(split(estimate), middle))
    a = dot(shared_t, d[...])
    a_hi[...], a_lo[...] = split(a)
    for step in range(1, NS_STEPS):
        middle = split(eye - 0.5 * dot3(inverse, estimate))
        inverse = split(dot3(middle, inverse))
        if step < NS_STEPS - 1:
            estimate = split(dot3(estimate, middle))
    root = 1.0 / jnp.sqrt(scale)
    stores = []
    width = 256
    for i in range(new.shape[1] // width):
        part = pl.ds(i * width, width)
        out = dot3(inverse, (a_hi[:, part], a_lo[:, part])) * root
        new[:, part] = out.astype(BF16)
        store = pltpu.make_async_copy(
            new.at[:, part], new_hbm.at[0, :, part], local_sem.at[1 + i]
        )
        store.start()
        stores.append(store)
    for copy in pending:
        copy.wait_send()
    for store in stores:
        store.wait()
    store_r.wait()


def solution(mesh):
    nz, ny, nx = mesh.shape["subj"], 8, 4
    names = ("subj", "y", "x", "core")
    return build(Mesh(mesh.devices.reshape(nz, ny, nx, 2), names))


def build(grid):
    vox = ("y", "x", "core")
    nz, ny, nx = (grid.shape[name] for name in ("subj", "y", "x"))
    block_z, block_y = HALF // nz, HALF // ny
    block = max(block_z, block_y)
    block_x = ROWS // nx
    copies = 4 + 3 * (nz - 1) + 3 * (ny - 1) + 6 * (nx - 1) + 2 * (ny - 1) + 4 * nx + 2 * (nz + ny)

    def shards(data, maps):
        _, trs, vectors = data.shape
        k = maps.shape[1]
        subjects = nz * data.shape[0]
        vmem = pltpu.VMEM
        response, new_maps = pl.pallas_call(
            functools.partial(kernel, (nz, ny, nx), subjects),
            name="srm_step",
            out_shape=(
                jax.ShapeDtypeStruct((trs, k), F32),
                jax.ShapeDtypeStruct((1, k, vectors), BF16),
            ),
            in_specs=[pl.BlockSpec(memory_space=pl.ANY)] * 2,
            out_specs=[pl.BlockSpec(memory_space=pl.ANY)] * 2,
            scratch_shapes=[
                vmem((ROWS, vectors), BF16),
                vmem((trs % 16, vectors), BF16),
                vmem((k, vectors), BF16),
                vmem((2, ROWS, LANES), F32),
                vmem((2, ROWS, LANES), F32),
                vmem((ROWS, LANES), F32),
                vmem((ROWS, LANES), F32),
                vmem((ROWS, LANES), F32),
                vmem((ROWS, LANES), F32),
                vmem((2, max(nz, ny) - 1, block, LANES), F32),
                vmem((nx - 1, block_x, LANES), F32),
                vmem((2, nx - 1, block // nx, LANES), F32),
                vmem((ny - 1, block_x // ny, LANES), F32),
                vmem((2, block, LANES), F32),
                vmem((block_x, LANES), F32),
                vmem((2, max(nz, ny), block // nx, LANES), F32),
                vmem((2, ROWS, LANES), F32),
                vmem((2, ROWS, LANES), F32),
                vmem((ROWS, ROWS), BF16),
                vmem((ROWS, ROWS), BF16),
                vmem((k, vectors), BF16),
                vmem((k, vectors), BF16),
                vmem((trs, k), F32),
                vmem((k, vectors), BF16),
                pltpu.SemaphoreType.DMA((8,)),
                pltpu.SemaphoreType.DMA((copies,)),
                pltpu.SemaphoreType.DMA((copies,)),
            ],
            compiler_params=pltpu.CompilerParams(
                collective_id=0, has_side_effects=True, vmem_limit_bytes=48 << 20
            ),
        )(data, maps)
        return response, new_maps

    return jax.shard_map(
        shards,
        mesh=grid,
        in_specs=(P("subj", None, vox), P("subj", None, vox)),
        out_specs=(P(), P("subj", None, vox)),
        check_vma=False,
    )
```

```python
import functools

import jax
import jax.numpy as jnp
from jax import lax
from jax.experimental import pallas as pl
from jax.experimental.pallas import tpu as pltpu
from jax.sharding import Mesh
from jax.sharding import PartitionSpec as P

NS_STEPS = 5
LANES = 128
ROWS = 512
CHUNKS = 2
HALF = ROWS // 2
MESH = pl.DeviceIdType.MESH
F32, BF16 = jnp.float32, jnp.bfloat16


def dot(a, b):
    return jnp.dot(a, b, preferred_element_type=F32)


def dot_nt(a, b):
    return lax.dot_general(a, b, (((1,), (1,)), ((), ())), preferred_element_type=F32)


def split(a):
    high = a.astype(BF16)
    return high, (a - high.astype(F32)).astype(BF16)


def dot3(a, b):
    ah, al = a
    bh, bl = b
    return dot(ah, bh) + (dot(ah, bl) + dot(al, bh))


def kernel(
    sizes,
    subjects,
    data_hbm,
    maps_hbm,
    p_hi,
    p_lo,
    a_hi,
    a_lo,
    resp,
    d,
    end,
    w,
    part_r,
    part_c,
    pair_r,
    pair_c,
    sum_r,
    sum_c,
    r1,
    c1,
    r2,
    c2,
    r2_sum,
    c2_sum,
    swap,
    full_r,
    full_c,
    gram_hi,
    gram_lo,
    local_sem,
    send_sem,
    recv_sem,
):
    nz, ny, nx = sizes
    trs = data_hbm.shape[1]
    me = {name: lax.axis_index(name) for name in ("subj", "y", "x", "core")}
    size = {"subj": nz, "y": ny, "x": nx, "core": 2}
    core = me["core"]
    other = 1 - core

    edge = trs // 16 * 16
    chunk = d.shape[1] // CHUNKS
    load_end = pltpu.make_async_copy(
        data_hbm.at[0, pl.ds(edge, trs - edge)], end, local_sem.at[2 * CHUNKS]
    )
    load_end.start()
    loads = []
    for i in range(CHUNKS):
        part = pl.ds(i * chunk, chunk)
        load_d = pltpu.make_async_copy(
            data_hbm.at[0, pl.ds(0, edge), part], d.at[pl.ds(0, edge), part], local_sem.at[2 * i]
        )
        load_w = pltpu.make_async_copy(
            maps_hbm.at[0, :, part], w.at[:, part], local_sem.at[2 * i + 1]
        )
        load_d.start()
        load_w.start()
        loads.append((part, load_d, load_w))

    barrier = pltpu.get_barrier_semaphore()
    partners = 0
    for axis, n in size.items():
        for s in range(1, n):
            pl.semaphore_signal(
                barrier,
                inc=1,
                device_id={axis: lax.rem(me[axis] + s, n)},
                device_id_type=MESH,
            )
            partners += 1

    pending = []

    def send(src, dst, axis, s, arrived):
        k = len(pending)
        copy = pltpu.make_async_remote_copy(
            src_ref=src,
            dst_ref=dst,
            send_sem=send_sem.at[k],
            recv_sem=recv_sem.at[k],
            device_id={axis: lax.rem(me[axis] + s, size[axis])},
            device_id_type=MESH,
        )
        copy.start()
        pending.append(copy)
        back = pltpu.make_async_remote_copy(
            src_ref=src,
            dst_ref=arrived,
            send_sem=send_sem.at[k],
            recv_sem=recv_sem.at[k],
            device_id={axis: lax.rem(me[axis] + s, size[axis])},
            device_id_type=MESH,
        )
        return back.wait_recv

    def near_first(n):
        return sorted(range(1, n), key=lambda s: min(s, n - s))

    def far_first(n):
        return near_first(n)[::-1]

    def ahead(axis, s):
        return lax.rem(me[axis] + s, size[axis])

    def behind(axis, s):
        return lax.rem(me[axis] + (size[axis] - s), size[axis])

    def rows(start, count):
        return pl.ds(pl.multiple_of(start, 8), count)

    zeros = jnp.zeros((LANES, LANES), F32)
    for slot in range(4):
        part_c[1, pl.ds(slot * LANES, LANES)] = zeros
    load_end.wait()
    d[pl.ds(edge, ROWS - edge), :] = jnp.concatenate(
        [end[...], jnp.zeros((ROWS - trs, d.shape[1]), BF16)], axis=0
    )
    partial = None
    for part, load_d, load_w in loads:
        load_d.wait()
        load_w.wait()
        term = dot_nt(d[:, part], w[:, part])
        partial = term if partial is None else partial + term
    part_r[0] = partial[:, :LANES]
    part_r[1] = partial[:, LANES:]
    pl.semaphore_wait(barrier, partners)
    got_pair_r = send(part_r.at[other], pair_r, "core", 1, pair_r)

    row = lax.broadcasted_iota(jnp.int32, (LANES, LANES), 0)
    col = lax.broadcasted_iota(jnp.int32, (LANES, LANES), 1)
    top = dot_nt(d[pl.ds(0, HALF), :], d[pl.ds(0, HALF), :])
    c00, c10, c11 = top[:LANES, :LANES], top[LANES:, :LANES], top[LANES:, LANES:]
    part_c[0, pl.ds(0, LANES)] = c10
    part_c[0, pl.ds(3 * LANES, LANES)] = jnp.where(row >= col, c00, c11)
    low = dot_nt(d[pl.ds(HALF, HALF), :], d[...])
    part_c[0, pl.ds(LANES, LANES)] = low[:LANES, :LANES]
    part_c[0, pl.ds(2 * LANES, LANES)] = low[:LANES, LANES : 2 * LANES]
    c22 = low[:LANES, 2 * LANES : 3 * LANES]
    c33 = low[LANES:, 3 * LANES :]
    last = 72
    for slot in range(3):
        part_c[1, pl.ds(slot * LANES, last)] = low[
            LANES : LANES + last, slot * LANES : (slot + 1) * LANES
        ]
    part_c[1, pl.ds(3 * LANES, LANES)] = jnp.where(row >= col, c22, c33)
    on_diagonal = row == col
    for slot, block in ((0, c11), (1, c33)):
        diagonal = jnp.sum(jnp.where(on_diagonal, block, 0.0), axis=0, keepdims=True)
        part_c[1, pl.ds(slot * LANES + 80, 8)] = jnp.broadcast_to(diagonal, (8, LANES))
    got_pair_c = send(part_c.at[other], pair_c, "core", 1, pair_c)

    lanes_of = (("subj", "y", 0), ("y", "subj", 1))
    got_pair_r()
    sum_r[...] = part_r[core] + pair_r[...]
    got = {}
    for axis, _, half in lanes_of:
        n = size[axis]
        block = HALF // n
        for s in far_first(n):
            got[half, s] = send(
                sum_r.at[rows(half * HALF + ahead(axis, s) * block, block)],
                r1.at[half, s - 1, pl.ds(0, block)],
                axis,
                s,
                r1.at[half, s - 1, pl.ds(0, block)],
            )
    got_pair_c()
    sum_c[...] = part_c[core] + pair_c[...]
    block_x = ROWS // nx
    for s in far_first(nx):
        got["c", s] = send(
            sum_c.at[rows(ahead("x", s) * block_x, block_x)], c1.at[s - 1], "x", s, c1.at[s - 1]
        )
    for axis, _, half in lanes_of:
        n = size[axis]
        block = HALF // n
        fine = block // nx
        total = sum_r[rows(half * HALF + me[axis] * block, block)]
        for s in near_first(n):
            got[half, s]()
            total = total + r1[half, s - 1, pl.ds(0, block)]
        r2_sum[half, pl.ds(0, block)] = total
        for s in far_first(nx):
            got[half, "x", s] = send(
                r2_sum.at[half, rows(ahead("x", s) * fine, fine)],
                r2.at[half, s - 1, pl.ds(0, fine)],
                "x",
                s,
                r2.at[half, s - 1, pl.ds(0, fine)],
            )
    total = sum_c[rows(me["x"] * block_x, block_x)]
    for s in near_first(nx):
        got["c", s]()
        total = total + c1[s - 1]
    c2_sum[...] = total
    fine_c = block_x // ny
    for s in far_first(ny):
        got["c", "y", s] = send(
            c2_sum.at[rows(ahead("y", s) * fine_c, fine_c)], c2.at[s - 1], "y", s, c2.at[s - 1]
        )
    for axis, across, half in lanes_of:
        fine = HALF // size[axis] // nx
        n = size[across]
        total = r2_sum[half, rows(me["x"] * fine, fine)]
        for s in near_first(nx):
            got[half, "x", s]()
            total = total + r2[half, s - 1, pl.ds(0, fine)]
        swap[half, me[across], pl.ds(0, fine)] = total
        for s in far_first(n):
            got[half, "swap", s] = send(
                swap.at[half, me[across], pl.ds(0, fine)],
                swap.at[half, me[across], pl.ds(0, fine)],
                across,
                s,
                swap.at[half, behind(across, s), pl.ds(0, fine)],
            )
    total = c2_sum[rows(me["y"] * fine_c, fine_c)]
    for s in near_first(ny):
        got["c", "y", s]()
        total = total + c2[s - 1]

    def gram_rows(x, y):
        return rows(x * block_x + y * fine_c, fine_c)

    mine = full_c.at[core, gram_rows(me["x"], me["y"])]
    mine[...] = total
    for s in far_first(ny):
        got["c", "ay", s] = send(
            mine, mine, "y", s, full_c.at[core, gram_rows(me["x"], behind("y", s))]
        )
    for axis, across, half in lanes_of:
        block = HALF // size[axis]
        fine = block // nx
        n = size[across]
        for s in near_first(n):
            got[half, "swap", s]()
        total = swap[half, 0, pl.ds(0, fine)]
        for i in range(1, n):
            total = total + swap[half, i, pl.ds(0, fine)]
        start = half * HALF + me[axis] * block
        mine = full_r.at[core, rows(start + me["x"] * fine, fine)]
        mine[...] = total * (1.0 / subjects)
        for s in far_first(nx):
            got[half, "ax", s] = send(
                mine, mine, "x", s, full_r.at[core, rows(start + behind("x", s) * fine, fine)]
            )
    for s in near_first(ny):
        got["c", "ay", s]()
    mine = full_c.at[core, rows(me["x"] * block_x, block_x)]
    for s in far_first(nx):
        got["c", "ax", s] = send(
            mine, mine, "x", s, full_c.at[core, rows(behind("x", s) * block_x, block_x)]
        )
    got_other_c = [
        send(mine, mine, "core", 1, full_c.at[other, rows(me["x"] * block_x, block_x)])
    ]
    got_other_r = []
    for axis, _, half in lanes_of:
        n = size[axis]
        block = HALF // n
        for s in near_first(nx):
            got[half, "ax", s]()
        here = rows(half * HALF + me[axis] * block, block)
        mine = full_r.at[core, here]
        for s in far_first(n):
            there = rows(half * HALF + behind(axis, s) * block, block)
            got[half, "az", s] = send(mine, mine, axis, s, full_r.at[core, there])
        got_other_r.append(send(mine, mine, "core", 1, full_r.at[other, here]))
    for s in near_first(nx):
        got["c", "ax", s]()
        here = rows(behind("x", s) * block_x, block_x)
        mine = full_c.at[core, here]
        got_other_c.append(send(mine, mine, "core", 1, full_c.at[other, here]))

    for s in near_first(max(nz, ny)):
        for axis, _, half in lanes_of:
            n = size[axis]
            if s >= n:
                continue
            block = HALF // n
            got[half, "az", s]()
            here = rows(half * HALF + behind(axis, s) * block, block)
            mine = full_r.at[core, here]
            got_other_r.append(send(mine, mine, "core", 1, full_r.at[other, here]))
    for wait in got_other_c:
        wait()

    def put(i, j, block):
        high, low_part = split(block)
        gram_hi[pl.ds(i * LANES, LANES), pl.ds(j * LANES, LANES)] = high
        gram_lo[pl.ds(i * LANES, LANES), pl.ds(j * LANES, LANES)] = low_part

    def put_both(i, j, block):
        put(i, j, block)
        put(j, i, block.T)

    put_both(1, 0, full_c[0, pl.ds(0, LANES)])
    put_both(2, 0, full_c[0, pl.ds(LANES, LANES)])
    put_both(2, 1, full_c[0, pl.ds(2 * LANES, LANES)])
    for slot in range(3):
        block = full_c[1, pl.ds(slot * LANES, LANES)]
        put_both(3, slot, jnp.where(row < last, block, 0.0))
    for half, i, j in ((0, 0, 1), (1, 2, 3)):
        packed = full_c[half, pl.ds(3 * LANES, LANES)]
        turned = packed.T
        diagonal = full_c[1, pl.ds(half * LANES + 80, 8)][:1]
        put(i, i, jnp.where(row >= col, packed, turned))
        block = jnp.where(row < col, packed, turned)
        put(j, j, jnp.where(on_diagonal, jnp.broadcast_to(diagonal, block.shape), block))

    for wait in got_other_r:
        wait()

    response = jnp.concatenate([full_r[0], full_r[1]], axis=1)
    resp[...] = response[:trs]
    shared = response.astype(BF16)
    shared_t = shared.T
    t_hi, t_lo = split(dot(shared_t, gram_hi[...]) + dot(shared_t, gram_lo[...]))
    gram = dot(t_hi, shared) + dot(t_lo, shared)
    k = gram.shape[0]

    scale = jnp.sqrt(jnp.sum(gram * gram, keepdims=True) + 1e-06)
    estimate = gram / scale
    unit = lax.broadcasted_iota(jnp.int32, (k, k), 0) == lax.broadcasted_iota(
        jnp.int32, (k, k), 1
    )
    eye = jnp.where(unit, 1.5, 0.0).astype(F32)
    middle = eye - 0.5 * estimate
    both = jnp.concatenate([dot3(split(estimate), split(middle)), middle], axis=0)
    a_hi[...], a_lo[...] = split(dot(shared_t, d[...]))
    for step in range(1, NS_STEPS):
        high, low_part = split(both)
        inverse = (high[k:], low_part[k:])
        middle = split(eye - 0.5 * dot3(inverse, (high[:k], low_part[:k])))
        if step < NS_STEPS - 1:
            both = dot3((high, low_part), middle)
    p_hi[...], p_lo[...] = split(dot3(inverse, middle) * (1.0 / jnp.sqrt(scale)))
    for copy in pending:
        copy.wait_send()


def finish(p_hi, p_lo, a_hi, a_lo, resp, resp_hbm, new_hbm, new, sem):
    store_r = pltpu.make_async_copy(resp, resp_hbm, sem.at[0])
    store_r.start()
    stores = []
    width = 256
    for i in range(new.shape[1] // width):
        part = pl.ds(i * width, width)
        out = dot3((p_hi[...], p_lo[...]), (a_hi[:, part], a_lo[:, part]))
        new[:, part] = out.astype(BF16)
        store = pltpu.make_async_copy(new.at[:, part], new_hbm.at[0, :, part], sem.at[1 + i])
        store.start()
        stores.append(store)
    for store in stores:
        store.wait()
    store_r.wait()


def solution(mesh):
    nz, ny, nx = mesh.shape["subj"], 8, 4
    names = ("subj", "y", "x", "core")
    return build(Mesh(mesh.devices.reshape(nz, ny, nx, 2), names))


def build(grid):
    vox = ("y", "x", "core")
    nz, ny, nx = (grid.shape[name] for name in ("subj", "y", "x"))
    block_z, block_y = HALF // nz, HALF // ny
    block = max(block_z, block_y)
    block_x = ROWS // nx
    copies = 4 + 3 * (nz - 1) + 3 * (ny - 1) + 6 * (nx - 1) + 2 * (ny - 1) + 4 * nx + 2 * (nz + ny)

    def shards(data, maps):
        _, trs, vectors = data.shape
        k = maps.shape[1]
        subjects = nz * data.shape[0]
        vmem = pltpu.VMEM
        held = pl.BlockSpec(memory_space=pltpu.VMEM)
        hbm = pl.BlockSpec(memory_space=pltpu.HBM)
        parts = pl.pallas_call(
            functools.partial(kernel, (nz, ny, nx), subjects),
            name="srm_step",
            out_shape=(
                jax.ShapeDtypeStruct((k, k), BF16),
                jax.ShapeDtypeStruct((k, k), BF16),
                jax.ShapeDtypeStruct((k, vectors), BF16),
                jax.ShapeDtypeStruct((k, vectors), BF16),
                jax.ShapeDtypeStruct((trs, k), F32),
            ),
            in_specs=[hbm] * 2,
            out_specs=[held] * 5,
            scratch_shapes=[
                vmem((ROWS, vectors), BF16),
                vmem((trs % 16, vectors), BF16),
                vmem((k, vectors), BF16),
                vmem((2, ROWS, LANES), F32),
                vmem((2, ROWS, LANES), F32),
                vmem((ROWS, LANES), F32),
                vmem((ROWS, LANES), F32),
                vmem((ROWS, LANES), F32),
                vmem((ROWS, LANES), F32),
                vmem((2, max(nz, ny) - 1, block, LANES), F32),
                vmem((nx - 1, block_x, LANES), F32),
                vmem((2, nx - 1, block // nx, LANES), F32),
                vmem((ny - 1, block_x // ny, LANES), F32),
                vmem((2, block, LANES), F32),
                vmem((block_x, LANES), F32),
                vmem((2, max(nz, ny), block // nx, LANES), F32),
                vmem((2, ROWS, LANES), F32),
                vmem((2, ROWS, LANES), F32),
                vmem((ROWS, ROWS), BF16),
                vmem((ROWS, ROWS), BF16),
                pltpu.SemaphoreType.DMA((2 * CHUNKS + 1,)),
                pltpu.SemaphoreType.DMA((copies,)),
                pltpu.SemaphoreType.DMA((copies,)),
            ],
            compiler_params=pltpu.CompilerParams(
                collective_id=0, has_side_effects=True, vmem_limit_bytes=54_550_000
            ),
        )(data, maps)
        return pl.pallas_call(
            finish,
            name="srm_maps",
            out_shape=(
                jax.ShapeDtypeStruct((trs, k), F32),
                jax.ShapeDtypeStruct((1, k, vectors), BF16),
            ),
            in_specs=[held] * 5,
            out_specs=[hbm] * 2,
            scratch_shapes=[vmem((k, vectors), BF16), pltpu.SemaphoreType.DMA((8,))],
            compiler_params=pltpu.CompilerParams(vmem_limit_bytes=16 << 20),
        )(*parts)

    return jax.shard_map(
        shards,
        mesh=grid,
        in_specs=(P("subj", None, vox), P("subj", None, vox)),
        out_specs=(P(), P("subj", None, vox)),
        check_vma=False,
    )
```

```python
import functools

import jax
import jax.numpy as jnp
from jax import lax
from jax.experimental import pallas as pl
from jax.experimental.pallas import tpu as pltpu
from jax.sharding import Mesh
from jax.sharding import PartitionSpec as P

NS_STEPS = 5
LANES = 128
ROWS = 512
CHUNKS = 2
LAG = 4
HALF = ROWS // 2
C_X = 256
SUMS = (
    ("r", 0, HALF, "subj", ("x", "y")),
    ("r", HALF, HALF, "y", ("x", "subj")),
    ("c", 0, C_X, "x", ("y",)),
    ("c", C_X, ROWS - C_X, "y", ("x",)),
)
MESH = pl.DeviceIdType.MESH
F32, BF16 = jnp.float32, jnp.bfloat16


def dot(a, b):
    return jnp.dot(a, b, preferred_element_type=F32)


def dot_nt(a, b):
    return lax.dot_general(a, b, (((1,), (1,)), ((), ())), preferred_element_type=F32)


def split(a):
    high = a.astype(BF16)
    return high, (a - high.astype(F32)).astype(BF16)


def dot3(a, b):
    ah, al = a
    bh, bl = b
    return dot(ah, bh) + (dot(ah, bl) + dot(al, bh))


def kernel(
    sizes,
    subjects,
    data_hbm,
    maps_hbm,
    p_hi,
    p_lo,
    a_hi,
    a_lo,
    resp,
    d,
    end,
    w,
    part_r,
    part_c,
    pair_r,
    pair_c,
    sum_r,
    sum_c,
    full_r,
    full_c,
    gram_hi,
    gram_lo,
    local_sem,
    send_sem,
    recv_sem,
    *buffers,
):
    nz, ny, nx = sizes
    trs = data_hbm.shape[1]
    me = {name: lax.axis_index(name) for name in ("subj", "y", "x", "core")}
    size = {"subj": nz, "y": ny, "x": nx, "core": 2}
    core = me["core"]
    other = 1 - core

    edge = trs // 16 * 16
    chunk = d.shape[1] // CHUNKS
    load_end = pltpu.make_async_copy(
        data_hbm.at[0, pl.ds(edge, trs - edge)], end, local_sem.at[2 * CHUNKS]
    )
    load_end.start()
    loads = []
    for i in range(CHUNKS):
        part = pl.ds(i * chunk, chunk)
        load_d = pltpu.make_async_copy(
            data_hbm.at[0, pl.ds(0, edge), part], d.at[pl.ds(0, edge), part], local_sem.at[2 * i]
        )
        load_w = pltpu.make_async_copy(
            maps_hbm.at[0, :, part], w.at[:, part], local_sem.at[2 * i + 1]
        )
        load_d.start()
        load_w.start()
        loads.append((part, load_d, load_w))

    barrier = pltpu.get_barrier_semaphore()
    partners = 0
    for axis, n in size.items():
        for s in range(1, n):
            pl.semaphore_signal(
                barrier,
                inc=1,
                device_id={axis: lax.rem(me[axis] + s, n)},
                device_id_type=MESH,
            )
            partners += 1

    pending = []

    def send(src, dst, axis, s, arrived):
        k = len(pending)
        copy = pltpu.make_async_remote_copy(
            src_ref=src,
            dst_ref=dst,
            send_sem=send_sem.at[k],
            recv_sem=recv_sem.at[k],
            device_id={axis: lax.rem(me[axis] + s, size[axis])},
            device_id_type=MESH,
        )
        copy.start()
        pending.append(copy)
        back = pltpu.make_async_remote_copy(
            src_ref=src,
            dst_ref=arrived,
            send_sem=send_sem.at[k],
            recv_sem=recv_sem.at[k],
            device_id={axis: lax.rem(me[axis] + s, size[axis])},
            device_id_type=MESH,
        )
        return back.wait_recv

    def nosend(*a):
        return lambda: None

    def near_first(n):
        return sorted(range(1, n), key=lambda s: min(s, n - s))

    def far_first(n):
        return near_first(n)[::-1]

    def ahead(axis, s):
        return lax.rem(me[axis] + s, size[axis])

    def behind(axis, s):
        return lax.rem(me[axis] + (size[axis] - s), size[axis])

    def rows(start, count):
        return pl.ds(pl.multiple_of(start, 8), count)

    zeros = jnp.zeros((LANES, LANES), F32)
    for slot in range(4):
        part_c[1, pl.ds(slot * LANES, LANES)] = zeros
    load_end.wait()
    d[pl.ds(edge, ROWS - edge), :] = jnp.concatenate(
        [end[...], jnp.zeros((ROWS - trs, d.shape[1]), BF16)], axis=0
    )
    partial = None
    for part, load_d, load_w in loads:
        load_d.wait()
        load_w.wait()
        term = dot_nt(d[:, part], w[:, part])
        partial = term if partial is None else partial + term
    part_r[0] = partial[:, :LANES]
    part_r[1] = partial[:, LANES:]
    pl.semaphore_wait(barrier, partners)
    got_pair_r = send(part_r.at[other], pair_r, "core", 1, pair_r)

    row = lax.broadcasted_iota(jnp.int32, (LANES, LANES), 0)
    col = lax.broadcasted_iota(jnp.int32, (LANES, LANES), 1)
    top = dot_nt(d[pl.ds(0, HALF), :], d[pl.ds(0, HALF), :])
    c00, c10, c11 = top[:LANES, :LANES], top[LANES:, :LANES], top[LANES:, LANES:]
    part_c[0, pl.ds(0, LANES)] = c10
    part_c[0, pl.ds(3 * LANES, LANES)] = jnp.where(row >= col, c00, c11)
    low = dot_nt(d[pl.ds(HALF, HALF), :], d[...])
    part_c[0, pl.ds(LANES, LANES)] = low[:LANES, :LANES]
    part_c[0, pl.ds(2 * LANES, LANES)] = low[:LANES, LANES : 2 * LANES]
    c22 = low[:LANES, 2 * LANES : 3 * LANES]
    c33 = low[LANES:, 3 * LANES :]
    last = 72
    for slot in range(3):
        part_c[1, pl.ds(slot * LANES, last)] = low[
            LANES : LANES + last, slot * LANES : (slot + 1) * LANES
        ]
    part_c[1, pl.ds(3 * LANES, LANES)] = jnp.where(row >= col, c22, c33)
    on_diagonal = row == col
    for slot, block in ((0, c11), (1, c33)):
        diagonal = jnp.sum(jnp.where(on_diagonal, block, 0.0), axis=0, keepdims=True)
        part_c[1, pl.ds(slot * LANES + 80, 8)] = jnp.broadcast_to(diagonal, (8, LANES))
    got_pair_c = send(part_c.at[other], pair_c, "core", 1, pair_c)

    got_other = {"r": [], "c": []}

    def summed(name, source, full, factor, start, count, axis, others, buffers):
        n = size[axis]
        block = count // n
        arrived, *swaps = buffers
        got = {}

        def place(at):
            return rows(start + at * block, block)

        for s in far_first(n):
            slot = arrived.at[s - 1]
            got[s] = send(source.at[place(ahead(axis, s))], slot, axis, s, slot)
        yield
        total = source[place(me[axis])]
        for s in far_first(n):
            got[s]()
            total = total + arrived[s - 1]
        for across, swap in zip(others, swaps):
            m = size[across]
            mine = swap.at[me[across]]
            mine[...] = total
            for s in far_first(m):
                got[s] = send(mine, mine, across, s, swap.at[behind(across, s)])
            yield
            for s in far_first(m):
                got[s]()
            total = swap[0]
            for i in range(1, m):
                total = total + swap[i]
        mine = full.at[core, place(me[axis])]
        mine[...] = total * factor
        for s in far_first(n):
            got[s] = send(mine, mine, axis, s, full.at[core, place(behind(axis, s))])
        yield
        for s in far_first(n):
            got[s]()
        here = rows(start, count)
        mine = full.at[core, here]
        got_other[name].append(send(mine, mine, "core", 1, full.at[other, here]))
        yield

    marks = []
    drained = 0

    def drain(upto):
        nonlocal drained
        for copy in pending[drained:upto]:
            copy.wait_send()
        drained = max(drained, upto)

    def step(*chains):
        for chain in chains:
            next(chain)
        marks.append(len(pending))
        if len(marks) > LAG:
            drain(marks[-1 - LAG])

    rest = iter(buffers)
    chains = []
    for name, start, count, axis, others in SUMS:
        source, full, factor = (
            (sum_r, full_r, 1.0 / subjects) if name == "r" else (sum_c, full_c, 1.0)
        )
        own = [next(rest) for _ in range(1 + len(others))]
        chains.append(summed(name, source, full, factor, start, count, axis, others, own))
    r0, r1, c0, c1 = chains
    got_pair_r()
    sum_r[...] = part_r[core] + pair_r[...]
    step(r0, r1)
    got_pair_c()
    sum_c[...] = part_c[core] + pair_c[...]
    step(c0, c1)
    step(c0)
    step(r0, r1)
    step(c1)
    step(r0, r1)
    step(c1)
    step(c0)
    step(r0, r1)
    step(c0, c1)
    step(r0, r1)
    for wait in got_other["c"]:
        wait()

    def put(i, j, block):
        high, low_part = split(block)
        gram_hi[pl.ds(i * LANES, LANES), pl.ds(j * LANES, LANES)] = high
        gram_lo[pl.ds(i * LANES, LANES), pl.ds(j * LANES, LANES)] = low_part

    def put_both(i, j, block):
        put(i, j, block)
        put(j, i, block.T)

    put_both(1, 0, full_c[0, pl.ds(0, LANES)])
    put_both(2, 0, full_c[0, pl.ds(LANES, LANES)])
    put_both(2, 1, full_c[0, pl.ds(2 * LANES, LANES)])
    for slot in range(3):
        block = full_c[1, pl.ds(slot * LANES, LANES)]
        put_both(3, slot, jnp.where(row < last, block, 0.0))
    for half, i, j in ((0, 0, 1), (1, 2, 3)):
        packed = full_c[half, pl.ds(3 * LANES, LANES)]
        turned = packed.T
        diagonal = full_c[1, pl.ds(half * LANES + 80, 8)][:1]
        put(i, i, jnp.where(row >= col, packed, turned))
        block = jnp.where(row < col, packed, turned)
        put(j, j, jnp.where(on_diagonal, jnp.broadcast_to(diagonal, block.shape), block))

    for wait in got_other["r"]:
        wait()

    response = jnp.concatenate([full_r[0], full_r[1]], axis=1)
    resp[...] = response[:trs]
    shared = response.astype(BF16)
    shared_t = shared.T
    t_hi, t_lo = split(dot(shared_t, gram_hi[...]) + dot(shared_t, gram_lo[...]))
    gram = dot(t_hi, shared) + dot(t_lo, shared)
    k = gram.shape[0]

    scale = jnp.sqrt(jnp.sum(gram * gram, keepdims=True) + 1e-06)
    estimate = gram / scale
    unit = lax.broadcasted_iota(jnp.int32, (k, k), 0) == lax.broadcasted_iota(
        jnp.int32, (k, k), 1
    )
    eye = jnp.where(unit, 1.5, 0.0).astype(F32)
    middle = eye - 0.5 * estimate
    both = jnp.concatenate([dot3(split(estimate), split(middle)), middle], axis=0)
    a_hi[...], a_lo[...] = split(dot(shared_t, d[...]))
    for step in range(1, NS_STEPS):
        high, low_part = split(both)
        inverse = (high[k:], low_part[k:])
        middle = split(eye - 0.5 * dot3(inverse, (high[:k], low_part[:k])))
        if step < NS_STEPS - 1:
            both = dot3((high, low_part), middle)
    p_hi[...], p_lo[...] = split(dot3(inverse, middle) * (1.0 / jnp.sqrt(scale)))
    drain(len(pending))


def finish(p_hi, p_lo, a_hi, a_lo, resp, resp_hbm, new_hbm, new, sem):
    store_r = pltpu.make_async_copy(resp, resp_hbm, sem.at[0])
    store_r.start()
    stores = []
    width = 256
    for i in range(new.shape[1] // width):
        part = pl.ds(i * width, width)
        out = dot3((p_hi[...], p_lo[...]), (a_hi[:, part], a_lo[:, part]))
        new[:, part] = out.astype(BF16)
        store = pltpu.make_async_copy(new.at[:, part], new_hbm.at[0, :, part], sem.at[1 + i])
        store.start()
        stores.append(store)
    for store in stores:
        store.wait()
    store_r.wait()


def solution(mesh):
    nz, ny, nx = mesh.shape["subj"], 8, 4
    names = ("subj", "y", "x", "core")
    return build(Mesh(mesh.devices.reshape(nz, ny, nx, 2), names))


def build(grid):
    vox = ("y", "x", "core")
    nz, ny, nx = (grid.shape[name] for name in ("subj", "y", "x"))
    size = {"subj": nz, "y": ny, "x": nx}
    shapes = []
    copies = 2
    for _, _, count, axis, others in SUMS:
        block = count // size[axis]
        shapes.append((size[axis] - 1, block, LANES))
        shapes += [(size[across], block, LANES) for across in others]
        copies += 2 * size[axis] - 1 + sum(size[across] - 1 for across in others)

    def shards(data, maps):
        _, trs, vectors = data.shape
        k = maps.shape[1]
        subjects = nz * data.shape[0]
        vmem = pltpu.VMEM
        held = pl.BlockSpec(memory_space=pltpu.VMEM)
        hbm = pl.BlockSpec(memory_space=pltpu.HBM)
        parts = pl.pallas_call(
            functools.partial(kernel, (nz, ny, nx), subjects),
            name="srm_step",
            out_shape=(
                jax.ShapeDtypeStruct((k, k), BF16),
                jax.ShapeDtypeStruct((k, k), BF16),
                jax.ShapeDtypeStruct((k, vectors), BF16),
                jax.ShapeDtypeStruct((k, vectors), BF16),
                jax.ShapeDtypeStruct((trs, k), F32),
            ),
            in_specs=[hbm] * 2,
            out_specs=[held] * 5,
            scratch_shapes=[
                vmem((ROWS, vectors), BF16),
                vmem((trs % 16, vectors), BF16),
                vmem((k, vectors), BF16),
                vmem((2, ROWS, LANES), F32),
                vmem((2, ROWS, LANES), F32),
                vmem((ROWS, LANES), F32),
                vmem((ROWS, LANES), F32),
                vmem((ROWS, LANES), F32),
                vmem((ROWS, LANES), F32),
                vmem((2, ROWS, LANES), F32),
                vmem((2, ROWS, LANES), F32),
                vmem((ROWS, ROWS), BF16),
                vmem((ROWS, ROWS), BF16),
                pltpu.SemaphoreType.DMA((2 * CHUNKS + 1,)),
                pltpu.SemaphoreType.DMA((copies,)),
                pltpu.SemaphoreType.DMA((copies,)),
                *(vmem(shape, F32) for shape in shapes),
            ],
            compiler_params=pltpu.CompilerParams(
                collective_id=0, has_side_effects=True, vmem_limit_bytes=54_550_000
            ),
        )(data, maps)
        return pl.pallas_call(
            finish,
            name="srm_maps",
            out_shape=(
                jax.ShapeDtypeStruct((trs, k), F32),
                jax.ShapeDtypeStruct((1, k, vectors), BF16),
            ),
            in_specs=[held] * 5,
            out_specs=[hbm] * 2,
            scratch_shapes=[vmem((k, vectors), BF16), pltpu.SemaphoreType.DMA((8,))],
            compiler_params=pltpu.CompilerParams(vmem_limit_bytes=16 << 20),
        )(*parts)

    return jax.shard_map(
        shards,
        mesh=grid,
        in_specs=(P("subj", None, vox), P("subj", None, vox)),
        out_specs=(P(), P("subj", None, vox)),
        check_vma=False,
    )
```

```python
import functools

import jax
import jax.numpy as jnp
from jax import lax
from jax.experimental import pallas as pl
from jax.experimental.pallas import tpu as pltpu
from jax.sharding import Mesh
from jax.sharding import PartitionSpec as P

NS_STEPS = 5
LANES = 128
ROWS = 512
CHUNKS = 4
LAG = 4
HALF = ROWS // 2
C_X = 256
SUMS = (
    ("r", 0, HALF, "subj", ("x", "y")),
    ("r", HALF, HALF, "y", ("x", "subj")),
    ("c", 0, C_X, "x", ("y",)),
    ("c", C_X, ROWS - C_X, "y", ("x",)),
)
MESH = pl.DeviceIdType.MESH
F32, BF16 = jnp.float32, jnp.bfloat16


def dot(a, b):
    return jnp.dot(a, b, preferred_element_type=F32)


def dot_nt(a, b):
    return lax.dot_general(a, b, (((1,), (1,)), ((), ())), preferred_element_type=F32)


def split(a):
    high = a.astype(BF16)
    return high, (a - high.astype(F32)).astype(BF16)


def dot3(a, b):
    ah, al = a
    bh, bl = b
    return dot(ah, bh) + (dot(ah, bl) + dot(al, bh))


def kernel(
    sizes,
    subjects,
    data_hbm,
    maps_hbm,
    p_hi,
    p_lo,
    a_hi,
    a_lo,
    resp,
    d,
    end,
    w,
    part_r,
    part_c,
    pair_r,
    pair_c,
    sum_r,
    sum_c,
    full_r,
    full_c,
    gram_hi,
    gram_lo,
    local_sem,
    send_sem,
    recv_sem,
    *buffers,
):
    nz, ny, nx = sizes
    trs = data_hbm.shape[1]
    me = {name: lax.axis_index(name) for name in ("subj", "y", "x", "core")}
    size = {"subj": nz, "y": ny, "x": nx, "core": 2}
    core = me["core"]
    other = 1 - core

    edge = trs // 16 * 16
    chunk = d.shape[1] // CHUNKS
    load_end = pltpu.make_async_copy(
        data_hbm.at[0, pl.ds(edge, trs - edge)], end, local_sem.at[2 * CHUNKS]
    )
    load_end.start()
    loads = []
    for i in range(CHUNKS):
        part = pl.ds(i * chunk, chunk)
        load_d = pltpu.make_async_copy(
            data_hbm.at[0, pl.ds(0, edge), part], d.at[pl.ds(0, edge), part], local_sem.at[2 * i]
        )
        load_w = pltpu.make_async_copy(
            maps_hbm.at[0, :, part], w.at[:, part], local_sem.at[2 * i + 1]
        )
        load_d.start()
        load_w.start()
        loads.append((part, load_d, load_w))

    barrier = pltpu.get_barrier_semaphore()
    partners = 0
    for axis, n in size.items():
        for s in range(1, n):
            pl.semaphore_signal(
                barrier,
                inc=1,
                device_id={axis: lax.rem(me[axis] + s, n)},
                device_id_type=MESH,
            )
            partners += 1

    pending = []

    def send(src, dst, axis, s, arrived):
        k = len(pending)
        copy = pltpu.make_async_remote_copy(
            src_ref=src,
            dst_ref=dst,
            send_sem=send_sem.at[k],
            recv_sem=recv_sem.at[k],
            device_id={axis: lax.rem(me[axis] + s, size[axis])},
            device_id_type=MESH,
        )
        copy.start()
        pending.append(copy)
        back = pltpu.make_async_remote_copy(
            src_ref=src,
            dst_ref=arrived,
            send_sem=send_sem.at[k],
            recv_sem=recv_sem.at[k],
            device_id={axis: lax.rem(me[axis] + s, size[axis])},
            device_id_type=MESH,
        )
        return back.wait_recv

    def nosend(*a):
        return lambda: None

    def near_first(n):
        return sorted(range(1, n), key=lambda s: min(s, n - s))

    def far_first(n):
        return near_first(n)[::-1]

    def ahead(axis, s):
        return lax.rem(me[axis] + s, size[axis])

    def behind(axis, s):
        return lax.rem(me[axis] + (size[axis] - s), size[axis])

    def rows(start, count):
        return pl.ds(pl.multiple_of(start, 8), count)

    zeros = jnp.zeros((LANES, LANES), F32)
    for slot in range(4):
        part_c[1, pl.ds(slot * LANES, LANES)] = zeros
    load_end.wait()
    d[pl.ds(edge, ROWS - edge), :] = jnp.concatenate(
        [end[...], jnp.zeros((ROWS - trs, d.shape[1]), BF16)], axis=0
    )
    partial = None
    for part, load_d, load_w in loads:
        load_d.wait()
        load_w.wait()
        term = dot_nt(d[:, part], w[:, part])
        partial = term if partial is None else partial + term
    part_r[0] = partial[:, :LANES]
    part_r[1] = partial[:, LANES:]
    pl.semaphore_wait(barrier, partners)
    got_pair_r = send(part_r.at[other], pair_r, "core", 1, pair_r)

    row = lax.broadcasted_iota(jnp.int32, (LANES, LANES), 0)
    col = lax.broadcasted_iota(jnp.int32, (LANES, LANES), 1)
    top = dot_nt(d[pl.ds(0, HALF), :], d[pl.ds(0, HALF), :])
    c00, c10, c11 = top[:LANES, :LANES], top[LANES:, :LANES], top[LANES:, LANES:]
    part_c[0, pl.ds(0, LANES)] = c10
    part_c[0, pl.ds(3 * LANES, LANES)] = jnp.where(row >= col, c00, c11)
    low = dot_nt(d[pl.ds(HALF, HALF), :], d[...])
    part_c[0, pl.ds(LANES, LANES)] = low[:LANES, :LANES]
    part_c[0, pl.ds(2 * LANES, LANES)] = low[:LANES, LANES : 2 * LANES]
    c22 = low[:LANES, 2 * LANES : 3 * LANES]
    c33 = low[LANES:, 3 * LANES :]
    last = 72
    for slot in range(3):
        part_c[1, pl.ds(slot * LANES, last)] = low[
            LANES : LANES + last, slot * LANES : (slot + 1) * LANES
        ]
    part_c[1, pl.ds(3 * LANES, LANES)] = jnp.where(row >= col, c22, c33)
    on_diagonal = row == col
    for slot, block in ((0, c11), (1, c33)):
        diagonal = jnp.sum(jnp.where(on_diagonal, block, 0.0), axis=0, keepdims=True)
        part_c[1, pl.ds(slot * LANES + 80, 8)] = jnp.broadcast_to(diagonal, (8, LANES))
    got_pair_c = send(part_c.at[other], pair_c, "core", 1, pair_c)

    got_other = {"r": [], "c": []}

    def summed(name, source, full, factor, start, count, axis, others, buffers):
        n = size[axis]
        block = count // n
        arrived, *swaps = buffers
        got = {}

        def place(at):
            return rows(start + at * block, block)

        for s in far_first(n):
            slot = arrived.at[s - 1]
            got[s] = send(source.at[place(ahead(axis, s))], slot, axis, s, slot)
        yield
        total = source[place(me[axis])]
        for s in far_first(n):
            got[s]()
            total = total + arrived[s - 1]
        for across, swap in zip(others, swaps):
            m = size[across]
            mine = swap.at[me[across]]
            mine[...] = total
            for s in far_first(m):
                got[s] = send(mine, mine, across, s, swap.at[behind(across, s)])
            yield
            for s in far_first(m):
                got[s]()
            total = swap[0]
            for i in range(1, m):
                total = total + swap[i]
        mine = full.at[core, place(me[axis])]
        mine[...] = total * factor
        for s in far_first(n):
            got[s] = send(mine, mine, axis, s, full.at[core, place(behind(axis, s))])
        yield
        for s in far_first(n):
            got[s]()
        here = rows(start, count)
        mine = full.at[core, here]
        got_other[name].append(send(mine, mine, "core", 1, full.at[other, here]))
        yield

    marks = []
    drained = 0

    def drain(upto):
        nonlocal drained
        for copy in pending[drained:upto]:
            copy.wait_send()
        drained = max(drained, upto)

    def step(*chains):
        for chain in chains:
            next(chain)
        marks.append(len(pending))
        if len(marks) > LAG:
            drain(marks[-1 - LAG])

    rest = iter(buffers)
    chains = []
    for name, start, count, axis, others in SUMS:
        source, full, factor = (
            (sum_r, full_r, 1.0 / subjects) if name == "r" else (sum_c, full_c, 1.0)
        )
        own = [next(rest) for _ in range(1 + len(others))]
        chains.append(summed(name, source, full, factor, start, count, axis, others, own))
    r0, r1, c0, c1 = chains
    got_pair_r()
    sum_r[...] = part_r[core] + pair_r[...]
    step(r0, r1)
    got_pair_c()
    sum_c[...] = part_c[core] + pair_c[...]
    step(c0, c1)
    step(c0)
    step(r0, r1)
    step(c1)
    step(r0, r1)
    step(c1)
    step(c0)
    step(r0, r1)
    step(c0, c1)
    step(r0, r1)
    for wait in got_other["c"]:
        wait()

    def put(i, j, block):
        high, low_part = split(block)
        gram_hi[pl.ds(i * LANES, LANES), pl.ds(j * LANES, LANES)] = high
        gram_lo[pl.ds(i * LANES, LANES), pl.ds(j * LANES, LANES)] = low_part

    def put_both(i, j, block):
        put(i, j, block)
        put(j, i, block.T)

    put_both(1, 0, full_c[0, pl.ds(0, LANES)])
    put_both(2, 0, full_c[0, pl.ds(LANES, LANES)])
    put_both(2, 1, full_c[0, pl.ds(2 * LANES, LANES)])
    for slot in range(3):
        block = full_c[1, pl.ds(slot * LANES, LANES)]
        put_both(3, slot, jnp.where(row < last, block, 0.0))
    for half, i, j in ((0, 0, 1), (1, 2, 3)):
        packed = full_c[half, pl.ds(3 * LANES, LANES)]
        turned = packed.T
        diagonal = full_c[1, pl.ds(half * LANES + 80, 8)][:1]
        put(i, i, jnp.where(row >= col, packed, turned))
        block = jnp.where(row < col, packed, turned)
        put(j, j, jnp.where(on_diagonal, jnp.broadcast_to(diagonal, block.shape), block))

    for wait in got_other["r"]:
        wait()

    response = jnp.concatenate([full_r[0], full_r[1]], axis=1)
    resp[...] = response[:trs]
    shared = response.astype(BF16)
    shared_t = shared.T
    t_hi, t_lo = split(dot(shared_t, gram_hi[...]) + dot(shared_t, gram_lo[...]))
    gram = dot(t_hi, shared) + dot(t_lo, shared)
    k = gram.shape[0]

    scale = jnp.sqrt(jnp.sum(gram * gram, keepdims=True) + 1e-06)
    estimate = gram / scale
    unit = lax.broadcasted_iota(jnp.int32, (k, k), 0) == lax.broadcasted_iota(
        jnp.int32, (k, k), 1
    )
    one = jnp.where(unit, 1.0, 0.0).astype(F32)
    split_x = split(estimate)
    product = None
    for step_pair in range(NS_STEPS // 2):
        x = estimate
        xs = split_x
        x2 = dot3(xs, xs)
        quartic = dot3(split(x2), split(0.0625 * x2 - 0.5625 * x))
        factor = split(2.25 * one - 2.4375 * x + 1.6875 * x2 + quartic)
        if product is None:
            a_hi[...], a_lo[...] = split(dot(shared_t, d[...]))
            xq = dot3(xs, factor)
            product = factor
        else:
            stacked = tuple(jnp.concatenate(pair, axis=0) for pair in zip(xs, product))
            both = dot3(stacked, factor)
            xq, product = both[:k], split(both[k:])
        estimate = dot3(split(xq), factor)
        split_x = split(estimate)
    if NS_STEPS % 2:
        inverse = dot3(split(1.5 * one - 0.5 * estimate), product)
    else:
        inverse = product[0].astype(F32) + product[1].astype(F32)
    p_hi[...], p_lo[...] = split(inverse * (1.0 / jnp.sqrt(scale)))
    drain(len(pending))


def finish(p_hi, p_lo, a_hi, a_lo, resp, resp_hbm, new_hbm, new, sem):
    store_r = pltpu.make_async_copy(resp, resp_hbm, sem.at[0])
    store_r.start()
    stores = []
    width = 256
    for i in range(new.shape[1] // width):
        part = pl.ds(i * width, width)
        out = dot3((p_hi[...], p_lo[...]), (a_hi[:, part], a_lo[:, part]))
        new[:, part] = out.astype(BF16)
        store = pltpu.make_async_copy(new.at[:, part], new_hbm.at[0, :, part], sem.at[1 + i])
        store.start()
        stores.append(store)
    for store in stores:
        store.wait()
    store_r.wait()


def solution(mesh):
    nz, ny, nx = mesh.shape["subj"], 8, 4
    names = ("subj", "y", "x", "core")
    return build(Mesh(mesh.devices.reshape(nz, ny, nx, 2), names))


def build(grid):
    vox = ("y", "x", "core")
    nz, ny, nx = (grid.shape[name] for name in ("subj", "y", "x"))
    size = {"subj": nz, "y": ny, "x": nx}
    shapes = []
    copies = 2
    for _, _, count, axis, others in SUMS:
        block = count // size[axis]
        shapes.append((size[axis] - 1, block, LANES))
        shapes += [(size[across], block, LANES) for across in others]
        copies += 2 * size[axis] - 1 + sum(size[across] - 1 for across in others)

    def shards(data, maps):
        _, trs, vectors = data.shape
        k = maps.shape[1]
        subjects = nz * data.shape[0]
        vmem = pltpu.VMEM
        held = pl.BlockSpec(memory_space=pltpu.VMEM)
        hbm = pl.BlockSpec(memory_space=pltpu.HBM)
        parts = pl.pallas_call(
            functools.partial(kernel, (nz, ny, nx), subjects),
            name="srm_step",
            out_shape=(
                jax.ShapeDtypeStruct((k, k), BF16),
                jax.ShapeDtypeStruct((k, k), BF16),
                jax.ShapeDtypeStruct((k, vectors), BF16),
                jax.ShapeDtypeStruct((k, vectors), BF16),
                jax.ShapeDtypeStruct((trs, k), F32),
            ),
            in_specs=[hbm] * 2,
            out_specs=[held] * 5,
            scratch_shapes=[
                vmem((ROWS, vectors), BF16),
                vmem((trs % 16, vectors), BF16),
                vmem((k, vectors), BF16),
                vmem((2, ROWS, LANES), F32),
                vmem((2, ROWS, LANES), F32),
                vmem((ROWS, LANES), F32),
                vmem((ROWS, LANES), F32),
                vmem((ROWS, LANES), F32),
                vmem((ROWS, LANES), F32),
                vmem((2, ROWS, LANES), F32),
                vmem((2, ROWS, LANES), F32),
                vmem((ROWS, ROWS), BF16),
                vmem((ROWS, ROWS), BF16),
                pltpu.SemaphoreType.DMA((2 * CHUNKS + 1,)),
                pltpu.SemaphoreType.DMA((copies,)),
                pltpu.SemaphoreType.DMA((copies,)),
                *(vmem(shape, F32) for shape in shapes),
            ],
            compiler_params=pltpu.CompilerParams(
                collective_id=0, has_side_effects=True, vmem_limit_bytes=54_550_000
            ),
        )(data, maps)
        return pl.pallas_call(
            finish,
            name="srm_maps",
            out_shape=(
                jax.ShapeDtypeStruct((trs, k), F32),
                jax.ShapeDtypeStruct((1, k, vectors), BF16),
            ),
            in_specs=[held] * 5,
            out_specs=[hbm] * 2,
            scratch_shapes=[vmem((k, vectors), BF16), pltpu.SemaphoreType.DMA((8,))],
            compiler_params=pltpu.CompilerParams(vmem_limit_bytes=16 << 20),
        )(*parts)

    return jax.shard_map(
        shards,
        mesh=grid,
        in_specs=(P("subj", None, vox), P("subj", None, vox)),
        out_specs=(P(), P("subj", None, vox)),
        check_vma=False,
    )
```

```python
import functools

import jax
import jax.numpy as jnp
from jax import lax
from jax.experimental import pallas as pl
from jax.experimental.pallas import tpu as pltpu
from jax.sharding import Mesh
from jax.sharding import PartitionSpec as P

NS_STEPS = 5
LANES = 128
ROWS = 512
CHUNKS = 4
LAG = 4
HALF = ROWS // 2
SUMS = (
    ("r", 0, HALF, "subj", ("x", "y")),
    ("r", HALF, HALF, "y", ("x", "subj")),
)
MESH = pl.DeviceIdType.MESH
F32, BF16 = jnp.float32, jnp.bfloat16


def dot(a, b):
    return jnp.dot(a, b, preferred_element_type=F32)


def dot_nt(a, b):
    return lax.dot_general(a, b, (((1,), (1,)), ((), ())), preferred_element_type=F32)


def split(a):
    high = a.astype(BF16)
    return high, (a - high.astype(F32)).astype(BF16)


def dot3(a, b):
    ah, al = a
    bh, bl = b
    return dot(ah, bh) + (dot(ah, bl) + dot(al, bh))


def kernel(
    sizes,
    subjects,
    data_hbm,
    maps_hbm,
    p_hi,
    p_lo,
    a_hi,
    a_lo,
    resp,
    d,
    end,
    w,
    part_r,
    part_c,
    pair_r,
    pair_c,
    sum_r,
    sum_c,
    full_r,
    full_c,
    gram_hi,
    gram_lo,
    local_sem,
    send_sem,
    recv_sem,
    *buffers,
):
    nz, ny, nx = sizes
    trs = data_hbm.shape[1]
    me = {name: lax.axis_index(name) for name in ("subj", "y", "x", "core")}
    size = {"subj": nz, "y": ny, "x": nx, "core": 2}
    core = me["core"]
    other = 1 - core

    edge = trs // 16 * 16
    chunk = d.shape[1] // CHUNKS
    load_end = pltpu.make_async_copy(
        data_hbm.at[0, pl.ds(edge, trs - edge)], end, local_sem.at[2 * CHUNKS]
    )
    load_end.start()
    loads = []
    for i in range(CHUNKS):
        part = pl.ds(i * chunk, chunk)
        load_d = pltpu.make_async_copy(
            data_hbm.at[0, pl.ds(0, edge), part], d.at[pl.ds(0, edge), part], local_sem.at[2 * i]
        )
        load_w = pltpu.make_async_copy(
            maps_hbm.at[0, :, part], w.at[:, part], local_sem.at[2 * i + 1]
        )
        load_d.start()
        load_w.start()
        loads.append((part, load_d, load_w))

    barrier = pltpu.get_barrier_semaphore()
    partners = 0
    for axis, n in size.items():
        for s in range(1, n):
            pl.semaphore_signal(
                barrier,
                inc=1,
                device_id={axis: lax.rem(me[axis] + s, n)},
                device_id_type=MESH,
            )
            partners += 1

    pending = []

    def send(src, dst, axis, s, arrived):
        k = len(pending)
        copy = pltpu.make_async_remote_copy(
            src_ref=src,
            dst_ref=dst,
            send_sem=send_sem.at[k],
            recv_sem=recv_sem.at[k],
            device_id={axis: lax.rem(me[axis] + s, size[axis])},
            device_id_type=MESH,
        )
        copy.start()
        pending.append(copy)
        back = pltpu.make_async_remote_copy(
            src_ref=src,
            dst_ref=arrived,
            send_sem=send_sem.at[k],
            recv_sem=recv_sem.at[k],
            device_id={axis: lax.rem(me[axis] + s, size[axis])},
            device_id_type=MESH,
        )
        return back.wait_recv

    def nosend(*a):
        return lambda: None

    def near_first(n):
        return sorted(range(1, n), key=lambda s: min(s, n - s))

    def far_first(n):
        return near_first(n)[::-1]

    def ahead(axis, s):
        return lax.rem(me[axis] + s, size[axis])

    def behind(axis, s):
        return lax.rem(me[axis] + (size[axis] - s), size[axis])

    def rows(start, count):
        return pl.ds(pl.multiple_of(start, 8), count)

    zeros = jnp.zeros((LANES, LANES), F32)
    for slot in range(4):
        part_c[1, pl.ds(slot * LANES, LANES)] = zeros
    load_end.wait()
    d[pl.ds(edge, ROWS - edge), :] = jnp.concatenate(
        [end[...], jnp.zeros((ROWS - trs, d.shape[1]), BF16)], axis=0
    )
    partial = None
    for part, load_d, load_w in loads:
        load_d.wait()
        load_w.wait()
        term = dot_nt(d[:, part], w[:, part])
        partial = term if partial is None else partial + term
    part_r[0] = partial[:, :LANES]
    part_r[1] = partial[:, LANES:]
    pl.semaphore_wait(barrier, partners)
    got_pair_r = send(part_r.at[other], pair_r, "core", 1, pair_r)

    row = lax.broadcasted_iota(jnp.int32, (LANES, LANES), 0)
    col = lax.broadcasted_iota(jnp.int32, (LANES, LANES), 1)
    top = dot_nt(d[pl.ds(0, HALF), :], d[pl.ds(0, HALF), :])
    c00, c10, c11 = top[:LANES, :LANES], top[LANES:, :LANES], top[LANES:, LANES:]
    part_c[0, pl.ds(0, LANES)] = c10
    part_c[0, pl.ds(3 * LANES, LANES)] = jnp.where(row >= col, c00, c11)
    low = dot_nt(d[pl.ds(HALF, HALF), :], d[...])
    part_c[0, pl.ds(LANES, LANES)] = low[:LANES, :LANES]
    part_c[0, pl.ds(2 * LANES, LANES)] = low[:LANES, LANES : 2 * LANES]
    c22 = low[:LANES, 2 * LANES : 3 * LANES]
    c33 = low[LANES:, 3 * LANES :]
    last = 72
    for slot in range(3):
        part_c[1, pl.ds(slot * LANES, last)] = low[
            LANES : LANES + last, slot * LANES : (slot + 1) * LANES
        ]
    part_c[1, pl.ds(3 * LANES, LANES)] = jnp.where(row >= col, c22, c33)
    on_diagonal = row == col
    for slot, block in ((0, c11), (1, c33)):
        diagonal = jnp.sum(jnp.where(on_diagonal, block, 0.0), axis=0, keepdims=True)
        part_c[1, pl.ds(slot * LANES + 80, 8)] = jnp.broadcast_to(diagonal, (8, LANES))
    got_pair_c = send(part_c.at[other], pair_c, "core", 1, pair_c)

    got_other = {"r": [], "c": []}

    def summed(name, source, full, factor, start, count, axis, others, buffers):
        n = size[axis]
        block = count // n
        arrived, *swaps = buffers
        got = {}

        def place(at):
            return rows(start + at * block, block)

        for s in far_first(n):
            slot = arrived.at[s - 1]
            got[s] = send(source.at[place(ahead(axis, s))], slot, axis, s, slot)
        yield
        total = source[place(me[axis])]
        for s in far_first(n):
            got[s]()
            total = total + arrived[s - 1]
        for across, swap in zip(others, swaps):
            m = size[across]
            mine = swap.at[me[across]]
            mine[...] = total
            for s in far_first(m):
                got[s] = send(mine, mine, across, s, swap.at[behind(across, s)])
            yield
            for s in far_first(m):
                got[s]()
            total = swap[0]
            for i in range(1, m):
                total = total + swap[i]
        mine = full.at[core, place(me[axis])]
        mine[...] = total * factor
        for s in far_first(n):
            got[s] = send(mine, mine, axis, s, full.at[core, place(behind(axis, s))])
        yield
        for s in far_first(n):
            got[s]()
        here = rows(start, count)
        mine = full.at[core, here]
        got_other[name].append(send(mine, mine, "core", 1, full.at[other, here]))
        yield

    block_x = ROWS // nx
    fine = block_x // ny

    def gram_sum(buffers):
        c1, c2_sum, c2 = buffers
        got = {}

        def place(x):
            return rows(x * block_x, block_x)

        def fine_place(x, y):
            return rows(x * block_x + y * fine, fine)

        for s in far_first(nx):
            slot = c1.at[s - 1]
            got[s] = send(sum_c.at[place(ahead("x", s))], slot, "x", s, slot)
        yield
        total = sum_c[place(me["x"])]
        for s in near_first(nx):
            got[s]()
            total = total + c1[s - 1]
        c2_sum[...] = total
        for s in far_first(ny):
            slot = c2.at[s - 1]
            got[s] = send(c2_sum.at[rows(ahead("y", s) * fine, fine)], slot, "y", s, slot)
        yield
        total = c2_sum[rows(me["y"] * fine, fine)]
        for s in far_first(ny):
            got[s]()
            total = total + c2[s - 1]
        mine = full_c.at[core, fine_place(me["x"], me["y"])]
        mine[...] = total
        for s in far_first(ny):
            there = full_c.at[core, fine_place(me["x"], behind("y", s))]
            got[s] = send(mine, mine, "y", s, there)
        yield
        for s in far_first(ny):
            got[s]()
        mine = full_c.at[core, place(me["x"])]
        for s in far_first(nx):
            got[s] = send(mine, mine, "x", s, full_c.at[core, place(behind("x", s))])
        yield
        for s in near_first(nx):
            got[s]()
        mine = full_c.at[core]
        got_other["c"].append(send(mine, mine, "core", 1, full_c.at[other]))
        yield

    marks = []
    drained = 0

    def drain(upto):
        nonlocal drained
        for copy in pending[drained:upto]:
            copy.wait_send()
        drained = max(drained, upto)

    def step(*chains):
        for chain in chains:
            next(chain)
        marks.append(len(pending))
        if len(marks) > LAG:
            drain(marks[-1 - LAG])

    rest = iter(buffers)
    chains = []
    for name, start, count, axis, others in SUMS:
        source, full, factor = (
            (sum_r, full_r, 1.0 / subjects) if name == "r" else (sum_c, full_c, 1.0)
        )
        own = [next(rest) for _ in range(1 + len(others))]
        chains.append(summed(name, source, full, factor, start, count, axis, others, own))
    r0, r1 = chains
    c0 = gram_sum(list(rest))
    got_pair_r()
    sum_r[...] = part_r[core] + pair_r[...]
    step(r0, r1)
    got_pair_c()
    sum_c[...] = part_c[core] + pair_c[...]
    step(c0)
    step(c0)
    step(r0, r1)
    step(r0, r1)
    step(c0)
    step(r0, r1)
    step(c0)
    step(r0, r1)
    step(c0)
    for wait in got_other["c"]:
        wait()

    def put(i, j, block):
        high, low_part = split(block)
        gram_hi[pl.ds(i * LANES, LANES), pl.ds(j * LANES, LANES)] = high
        gram_lo[pl.ds(i * LANES, LANES), pl.ds(j * LANES, LANES)] = low_part

    def put_both(i, j, block):
        put(i, j, block)
        put(j, i, block.T)

    put_both(1, 0, full_c[0, pl.ds(0, LANES)])
    put_both(2, 0, full_c[0, pl.ds(LANES, LANES)])
    put_both(2, 1, full_c[0, pl.ds(2 * LANES, LANES)])
    for slot in range(3):
        block = full_c[1, pl.ds(slot * LANES, LANES)]
        put_both(3, slot, jnp.where(row < last, block, 0.0))
    for half, i, j in ((0, 0, 1), (1, 2, 3)):
        packed = full_c[half, pl.ds(3 * LANES, LANES)]
        turned = packed.T
        diagonal = full_c[1, pl.ds(half * LANES + 80, 8)][:1]
        put(i, i, jnp.where(row >= col, packed, turned))
        block = jnp.where(row < col, packed, turned)
        put(j, j, jnp.where(on_diagonal, jnp.broadcast_to(diagonal, block.shape), block))

    for wait in got_other["r"]:
        wait()

    response = jnp.concatenate([full_r[0], full_r[1]], axis=1)
    resp[...] = response[:trs]
    shared = response.astype(BF16)
    shared_t = shared.T
    t_hi, t_lo = split(dot(shared_t, gram_hi[...]) + dot(shared_t, gram_lo[...]))
    gram = dot(t_hi, shared) + dot(t_lo, shared)
    k = gram.shape[0]

    scale = jnp.sqrt(jnp.sum(gram * gram, keepdims=True) + 1e-06)
    estimate = gram / scale
    unit = lax.broadcasted_iota(jnp.int32, (k, k), 0) == lax.broadcasted_iota(
        jnp.int32, (k, k), 1
    )
    one = jnp.where(unit, 1.0, 0.0).astype(F32)
    split_x = split(estimate)
    product = None
    for step_pair in range(NS_STEPS // 2):
        x = estimate
        xs = split_x
        x2 = dot3(xs, xs)
        quartic = dot3(split(x2), split(0.0625 * x2 - 0.5625 * x))
        factor = split(2.25 * one - 2.4375 * x + 1.6875 * x2 + quartic)
        if product is None:
            a_hi[...], a_lo[...] = split(dot(shared_t, d[...]))
            xq = dot3(xs, factor)
            product = factor
        else:
            stacked = tuple(jnp.concatenate(pair, axis=0) for pair in zip(xs, product))
            both = dot3(stacked, factor)
            xq, product = both[:k], split(both[k:])
        estimate = dot3(split(xq), factor)
        split_x = split(estimate)
    if NS_STEPS % 2:
        inverse = dot3(split(1.5 * one - 0.5 * estimate), product)
    else:
        inverse = product[0].astype(F32) + product[1].astype(F32)
    p_hi[...], p_lo[...] = split(inverse * (1.0 / jnp.sqrt(scale)))
    drain(len(pending))


def finish(p_hi, p_lo, a_hi, a_lo, resp, resp_hbm, new_hbm, new, sem):
    store_r = pltpu.make_async_copy(resp, resp_hbm, sem.at[0])
    store_r.start()
    stores = []
    width = 256
    for i in range(new.shape[1] // width):
        part = pl.ds(i * width, width)
        out = dot3((p_hi[...], p_lo[...]), (a_hi[:, part], a_lo[:, part]))
        new[:, part] = out.astype(BF16)
        store = pltpu.make_async_copy(new.at[:, part], new_hbm.at[0, :, part], sem.at[1 + i])
        store.start()
        stores.append(store)
    for store in stores:
        store.wait()
    store_r.wait()


def solution(mesh):
    nz, ny, nx = mesh.shape["subj"], 8, 4
    names = ("subj", "y", "x", "core")
    return build(Mesh(mesh.devices.reshape(nz, ny, nx, 2), names))


def build(grid):
    vox = ("y", "x", "core")
    nz, ny, nx = (grid.shape[name] for name in ("subj", "y", "x"))
    size = {"subj": nz, "y": ny, "x": nx}
    shapes = []
    copies = 2
    for _, _, count, axis, others in SUMS:
        block = count // size[axis]
        shapes.append((size[axis] - 1, block, LANES))
        shapes += [(size[across], block, LANES) for across in others]
        copies += 2 * size[axis] - 1 + sum(size[across] - 1 for across in others)
    block_x = ROWS // nx
    shapes += [(nx - 1, block_x, LANES), (block_x, LANES), (ny - 1, block_x // ny, LANES)]
    copies += 2 * (nx + ny)

    def shards(data, maps):
        _, trs, vectors = data.shape
        k = maps.shape[1]
        subjects = nz * data.shape[0]
        vmem = pltpu.VMEM
        held = pl.BlockSpec(memory_space=pltpu.VMEM)
        hbm = pl.BlockSpec(memory_space=pltpu.HBM)
        parts = pl.pallas_call(
            functools.partial(kernel, (nz, ny, nx), subjects),
            name="srm_step",
            out_shape=(
                jax.ShapeDtypeStruct((k, k), BF16),
                jax.ShapeDtypeStruct((k, k), BF16),
                jax.ShapeDtypeStruct((k, vectors), BF16),
                jax.ShapeDtypeStruct((k, vectors), BF16),
                jax.ShapeDtypeStruct((trs, k), F32),
            ),
            in_specs=[hbm] * 2,
            out_specs=[held] * 5,
            scratch_shapes=[
                vmem((ROWS, vectors), BF16),
                vmem((trs % 16, vectors), BF16),
                vmem((k, vectors), BF16),
                vmem((2, ROWS, LANES), F32),
                vmem((2, ROWS, LANES), F32),
                vmem((ROWS, LANES), F32),
                vmem((ROWS, LANES), F32),
                vmem((ROWS, LANES), F32),
                vmem((ROWS, LANES), F32),
                vmem((2, ROWS, LANES), F32),
                vmem((2, ROWS, LANES), F32),
                vmem((ROWS, ROWS), BF16),
                vmem((ROWS, ROWS), BF16),
                pltpu.SemaphoreType.DMA((2 * CHUNKS + 1,)),
                pltpu.SemaphoreType.DMA((copies,)),
                pltpu.SemaphoreType.DMA((copies,)),
                *(vmem(shape, F32) for shape in shapes),
            ],
            compiler_params=pltpu.CompilerParams(
                collective_id=0, has_side_effects=True, vmem_limit_bytes=54_550_000
            ),
        )(data, maps)
        return pl.pallas_call(
            finish,
            name="srm_maps",
            out_shape=(
                jax.ShapeDtypeStruct((trs, k), F32),
                jax.ShapeDtypeStruct((1, k, vectors), BF16),
            ),
            in_specs=[held] * 5,
            out_specs=[hbm] * 2,
            scratch_shapes=[vmem((k, vectors), BF16), pltpu.SemaphoreType.DMA((8,))],
            compiler_params=pltpu.CompilerParams(vmem_limit_bytes=16 << 20),
        )(*parts)

    return jax.shard_map(
        shards,
        mesh=grid,
        in_specs=(P("subj", None, vox), P("subj", None, vox)),
        out_specs=(P(), P("subj", None, vox)),
        check_vma=False,
    )
```

```python
import functools

import jax
import jax.numpy as jnp
from jax import lax
from jax.experimental import pallas as pl
from jax.experimental.pallas import tpu as pltpu
from jax.sharding import Mesh
from jax.sharding import PartitionSpec as P

NS_STEPS = 5
LANES = 128
ROWS = 512
CHUNKS = 4
LAG = 4
HALF = ROWS // 2
SUMS = (
    ("r", 0, HALF, "subj", ("x", "y")),
    ("r", HALF, HALF, "y", ("x", "subj")),
)
MESH = pl.DeviceIdType.MESH
F32, BF16 = jnp.float32, jnp.bfloat16


def dot(a, b):
    return jnp.dot(a, b, preferred_element_type=F32)


def dot_nt(a, b):
    return lax.dot_general(a, b, (((1,), (1,)), ((), ())), preferred_element_type=F32)


def split(a):
    high = a.astype(BF16)
    return high, (a - high.astype(F32)).astype(BF16)


def dot3(a, b):
    ah, al = a
    bh, bl = b
    return dot(ah, bh) + (dot(ah, bl) + dot(al, bh))


def kernel(
    sizes,
    subjects,
    data_hbm,
    maps_hbm,
    p_hi,
    p_lo,
    a_hi,
    a_lo,
    resp,
    d,
    end,
    w,
    part_r,
    part_c,
    pair_r,
    pair_c,
    sum_r,
    sum_c,
    full_r,
    full_c,
    gram_hi,
    gram_lo,
    local_sem,
    send_sem,
    recv_sem,
    *buffers,
):
    nz, ny, nx = sizes
    trs = data_hbm.shape[1]
    me = {name: lax.axis_index(name) for name in ("subj", "y", "x", "core")}
    size = {"subj": nz, "y": ny, "x": nx, "core": 2}
    core = me["core"]
    other = 1 - core

    edge = trs // 16 * 16
    chunk = d.shape[1] // CHUNKS
    load_end = pltpu.make_async_copy(
        data_hbm.at[0, pl.ds(edge, trs - edge)], end, local_sem.at[2 * CHUNKS]
    )
    load_end.start()
    loads = []
    for i in range(CHUNKS):
        part = pl.ds(i * chunk, chunk)
        load_d = pltpu.make_async_copy(
            data_hbm.at[0, pl.ds(0, edge), part], d.at[pl.ds(0, edge), part], local_sem.at[2 * i]
        )
        load_w = pltpu.make_async_copy(
            maps_hbm.at[0, :, part], w.at[:, part], local_sem.at[2 * i + 1]
        )
        load_d.start()
        load_w.start()
        loads.append((part, load_d, load_w))

    barrier = pltpu.get_barrier_semaphore()
    partners = sorted(
        ((axis, s) for axis, n in size.items() for s in range(1, n)),
        key=lambda p: -min(p[1], size[p[0]] - p[1]),
    )
    for axis, s in partners:
        pl.semaphore_signal(
            barrier,
            inc=1,
            device_id={axis: lax.rem(me[axis] + s, size[axis])},
            device_id_type=MESH,
        )

    pending = []

    def send(src, dst, axis, s, arrived):
        k = len(pending)
        copy = pltpu.make_async_remote_copy(
            src_ref=src,
            dst_ref=dst,
            send_sem=send_sem.at[k],
            recv_sem=recv_sem.at[k],
            device_id={axis: lax.rem(me[axis] + s, size[axis])},
            device_id_type=MESH,
        )
        copy.start()
        pending.append(copy)
        back = pltpu.make_async_remote_copy(
            src_ref=src,
            dst_ref=arrived,
            send_sem=send_sem.at[k],
            recv_sem=recv_sem.at[k],
            device_id={axis: lax.rem(me[axis] + s, size[axis])},
            device_id_type=MESH,
        )
        return back.wait_recv

    def nosend(*a):
        return lambda: None

    def near_first(n):
        return sorted(range(1, n), key=lambda s: min(s, n - s))

    def far_first(n):
        return near_first(n)[::-1]

    def ahead(axis, s):
        return lax.rem(me[axis] + s, size[axis])

    def behind(axis, s):
        return lax.rem(me[axis] + (size[axis] - s), size[axis])

    def rows(start, count):
        return pl.ds(pl.multiple_of(start, 8), count)

    zeros = jnp.zeros((LANES, LANES), F32)
    for slot in range(4):
        part_c[1, pl.ds(slot * LANES, LANES)] = zeros
    load_end.wait()
    d[pl.ds(edge, ROWS - edge), :] = jnp.concatenate(
        [end[...], jnp.zeros((ROWS - trs, d.shape[1]), BF16)], axis=0
    )
    partial = None
    for part, load_d, load_w in loads:
        load_d.wait()
        load_w.wait()
        term = dot_nt(d[:, part], w[:, part])
        partial = term if partial is None else partial + term
    part_r[0] = partial[:, :LANES]
    part_r[1] = partial[:, LANES:]
    pl.semaphore_wait(barrier, len(partners))
    got_pair_r = send(part_r.at[other], pair_r, "core", 1, pair_r)

    row = lax.broadcasted_iota(jnp.int32, (LANES, LANES), 0)
    col = lax.broadcasted_iota(jnp.int32, (LANES, LANES), 1)
    top = dot_nt(d[pl.ds(0, HALF), :], d[pl.ds(0, HALF), :])
    c00, c10, c11 = top[:LANES, :LANES], top[LANES:, :LANES], top[LANES:, LANES:]
    part_c[0, pl.ds(0, LANES)] = c10
    part_c[0, pl.ds(3 * LANES, LANES)] = jnp.where(row >= col, c00, c11)
    low = dot_nt(d[pl.ds(HALF, HALF), :], d[...])
    part_c[0, pl.ds(LANES, LANES)] = low[:LANES, :LANES]
    part_c[0, pl.ds(2 * LANES, LANES)] = low[:LANES, LANES : 2 * LANES]
    c22 = low[:LANES, 2 * LANES : 3 * LANES]
    c33 = low[LANES:, 3 * LANES :]
    last = 72
    for slot in range(3):
        part_c[1, pl.ds(slot * LANES, last)] = low[
            LANES : LANES + last, slot * LANES : (slot + 1) * LANES
        ]
    part_c[1, pl.ds(3 * LANES, LANES)] = jnp.where(row >= col, c22, c33)
    on_diagonal = row == col
    for slot, block in ((0, c11), (1, c33)):
        diagonal = jnp.sum(jnp.where(on_diagonal, block, 0.0), axis=0, keepdims=True)
        part_c[1, pl.ds(slot * LANES + 80, 8)] = jnp.broadcast_to(diagonal, (8, LANES))
    got_pair_c = send(part_c.at[other], pair_c, "core", 1, pair_c)

    got_other = {"r": [], "c": []}

    def summed(name, source, full, factor, start, count, axis, others, buffers):
        n = size[axis]
        block = count // n
        arrived, *swaps = buffers
        got = {}

        def place(at):
            return rows(start + at * block, block)

        for s in far_first(n):
            slot = arrived.at[s - 1]
            got[s] = send(source.at[place(ahead(axis, s))], slot, axis, s, slot)
        yield
        total = source[place(me[axis])]
        for s in far_first(n):
            got[s]()
            total = total + arrived[s - 1]
        for across, swap in zip(others, swaps):
            m = size[across]
            mine = swap.at[me[across]]
            mine[...] = total
            for s in far_first(m):
                got[s] = send(mine, mine, across, s, swap.at[behind(across, s)])
            yield
            for s in far_first(m):
                got[s]()
            total = swap[0]
            for i in range(1, m):
                total = total + swap[i]
        mine = full.at[core, place(me[axis])]
        mine[...] = total * factor
        for s in far_first(n):
            got[s] = send(mine, mine, axis, s, full.at[core, place(behind(axis, s))])
        yield
        for s in far_first(n):
            got[s]()
        here = rows(start, count)
        mine = full.at[core, here]
        got_other[name].append(send(mine, mine, "core", 1, full.at[other, here]))
        yield

    block_x = ROWS // nx
    fine = block_x // ny

    def gram_sum(buffers):
        c1, c2_sum, c2 = buffers
        got = {}

        def place(x):
            return rows(x * block_x, block_x)

        def fine_place(x, y):
            return rows(x * block_x + y * fine, fine)

        for s in far_first(nx):
            slot = c1.at[s - 1]
            got[s] = send(sum_c.at[place(ahead("x", s))], slot, "x", s, slot)
        yield
        total = sum_c[place(me["x"])]
        for s in near_first(nx):
            got[s]()
            total = total + c1[s - 1]
        c2_sum[...] = total
        for s in far_first(ny):
            slot = c2.at[s - 1]
            got[s] = send(c2_sum.at[rows(ahead("y", s) * fine, fine)], slot, "y", s, slot)
        yield
        total = c2_sum[rows(me["y"] * fine, fine)]
        for s in far_first(ny):
            got[s]()
            total = total + c2[s - 1]
        mine = full_c.at[core, fine_place(me["x"], me["y"])]
        mine[...] = total
        for s in far_first(ny):
            there = full_c.at[core, fine_place(me["x"], behind("y", s))]
            got[s] = send(mine, mine, "y", s, there)
        yield
        for s in far_first(ny):
            got[s]()
        mine = full_c.at[core, place(me["x"])]
        for s in far_first(nx):
            got[s] = send(mine, mine, "x", s, full_c.at[core, place(behind("x", s))])
        yield
        for s in near_first(nx):
            got[s]()
        mine = full_c.at[core]
        got_other["c"].append(send(mine, mine, "core", 1, full_c.at[other]))
        yield

    marks = []
    drained = 0

    def drain(upto):
        nonlocal drained
        for copy in pending[drained:upto]:
            copy.wait_send()
        drained = max(drained, upto)

    def step(*chains):
        for chain in chains:
            next(chain)
        marks.append(len(pending))
        if len(marks) > LAG:
            drain(marks[-1 - LAG])

    rest = iter(buffers)
    chains = []
    for name, start, count, axis, others in SUMS:
        source, full, factor = (
            (sum_r, full_r, 1.0 / subjects) if name == "r" else (sum_c, full_c, 1.0)
        )
        own = [next(rest) for _ in range(1 + len(others))]
        chains.append(summed(name, source, full, factor, start, count, axis, others, own))
    r0, r1 = chains
    c0 = gram_sum(list(rest))
    got_pair_r()
    sum_r[...] = part_r[core] + pair_r[...]
    step(r0, r1)
    got_pair_c()
    sum_c[...] = part_c[core] + pair_c[...]
    step(c0)
    step(c0)
    step(r0, r1)
    step(r0, r1)
    step(c0)
    step(r0, r1)
    step(c0)
    step(r0, r1)
    step(c0)
    for wait in got_other["c"]:
        wait()

    def put(i, j, block):
        high, low_part = split(block)
        gram_hi[pl.ds(i * LANES, LANES), pl.ds(j * LANES, LANES)] = high
        gram_lo[pl.ds(i * LANES, LANES), pl.ds(j * LANES, LANES)] = low_part

    def put_both(i, j, block):
        put(i, j, block)
        put(j, i, block.T)

    put_both(1, 0, full_c[0, pl.ds(0, LANES)])
    put_both(2, 0, full_c[0, pl.ds(LANES, LANES)])
    put_both(2, 1, full_c[0, pl.ds(2 * LANES, LANES)])
    for slot in range(3):
        block = full_c[1, pl.ds(slot * LANES, LANES)]
        put_both(3, slot, jnp.where(row < last, block, 0.0))
    for half, i, j in ((0, 0, 1), (1, 2, 3)):
        packed = full_c[half, pl.ds(3 * LANES, LANES)]
        turned = packed.T
        diagonal = full_c[1, pl.ds(half * LANES + 80, 8)][:1]
        put(i, i, jnp.where(row >= col, packed, turned))
        block = jnp.where(row < col, packed, turned)
        put(j, j, jnp.where(on_diagonal, jnp.broadcast_to(diagonal, block.shape), block))

    for wait in got_other["r"]:
        wait()

    response = jnp.concatenate([full_r[0], full_r[1]], axis=1)
    resp[...] = response[:trs]
    shared = response.astype(BF16)
    shared_t = shared.T
    t_hi, t_lo = split(dot(shared_t, gram_hi[...]) + dot(shared_t, gram_lo[...]))
    gram = dot(t_hi, shared) + dot(t_lo, shared)
    k = gram.shape[0]

    scale = jnp.sqrt(jnp.sum(gram * gram, keepdims=True) + 1e-06)
    estimate = gram / scale
    unit = lax.broadcasted_iota(jnp.int32, (k, k), 0) == lax.broadcasted_iota(
        jnp.int32, (k, k), 1
    )
    one = jnp.where(unit, 1.0, 0.0).astype(F32)
    split_x = split(estimate)
    product = None
    for step_pair in range(NS_STEPS // 2):
        x = estimate
        xs = split_x
        x2 = dot3(xs, xs)
        quartic = dot3(split(x2), split(0.0625 * x2 - 0.5625 * x))
        factor = split(2.25 * one - 2.4375 * x + 1.6875 * x2 + quartic)
        if product is None:
            a_hi[...], a_lo[...] = split(dot(shared_t, d[...]))
            xq = dot3(xs, factor)
            product = factor
        else:
            stacked = tuple(jnp.concatenate(pair, axis=0) for pair in zip(xs, product))
            both = dot3(stacked, factor)
            xq, product = both[:k], split(both[k:])
        estimate = dot3(split(xq), factor)
        split_x = split(estimate)
    if NS_STEPS % 2:
        inverse = dot3(split(1.5 * one - 0.5 * estimate), product)
    else:
        inverse = product[0].astype(F32) + product[1].astype(F32)
    p_hi[...], p_lo[...] = split(inverse * (1.0 / jnp.sqrt(scale)))
    drain(len(pending))


def finish(p_hi, p_lo, a_hi, a_lo, resp, resp_hbm, new_hbm, new, sem):
    store_r = pltpu.make_async_copy(resp, resp_hbm, sem.at[0])
    store_r.start()
    stores = []
    width = 256
    for i in range(new.shape[1] // width):
        part = pl.ds(i * width, width)
        out = dot3((p_hi[...], p_lo[...]), (a_hi[:, part], a_lo[:, part]))
        new[:, part] = out.astype(BF16)
        store = pltpu.make_async_copy(new.at[:, part], new_hbm.at[0, :, part], sem.at[1 + i])
        store.start()
        stores.append(store)
    for store in stores:
        store.wait()
    store_r.wait()


def solution(mesh):
    nz, ny, nx = mesh.shape["subj"], 8, 4
    names = ("subj", "y", "x", "core")
    return build(Mesh(mesh.devices.reshape(nz, ny, nx, 2), names))


def build(grid):
    vox = ("y", "x", "core")
    nz, ny, nx = (grid.shape[name] for name in ("subj", "y", "x"))
    size = {"subj": nz, "y": ny, "x": nx}
    shapes = []
    copies = 2
    for _, _, count, axis, others in SUMS:
        block = count // size[axis]
        shapes.append((size[axis] - 1, block, LANES))
        shapes += [(size[across], block, LANES) for across in others]
        copies += 2 * size[axis] - 1 + sum(size[across] - 1 for across in others)
    block_x = ROWS // nx
    shapes += [(nx - 1, block_x, LANES), (block_x, LANES), (ny - 1, block_x // ny, LANES)]
    copies += 2 * (nx + ny)

    def shards(data, maps):
        _, trs, vectors = data.shape
        k = maps.shape[1]
        subjects = nz * data.shape[0]
        vmem = pltpu.VMEM
        held = pl.BlockSpec(memory_space=pltpu.VMEM)
        hbm = pl.BlockSpec(memory_space=pltpu.HBM)
        parts = pl.pallas_call(
            functools.partial(kernel, (nz, ny, nx), subjects),
            name="srm_step",
            out_shape=(
                jax.ShapeDtypeStruct((k, k), BF16),
                jax.ShapeDtypeStruct((k, k), BF16),
                jax.ShapeDtypeStruct((k, vectors), BF16),
                jax.ShapeDtypeStruct((k, vectors), BF16),
                jax.ShapeDtypeStruct((trs, k), F32),
            ),
            in_specs=[hbm] * 2,
            out_specs=[held] * 5,
            scratch_shapes=[
                vmem((ROWS, vectors), BF16),
                vmem((trs % 16, vectors), BF16),
                vmem((k, vectors), BF16),
                vmem((2, ROWS, LANES), F32),
                vmem((2, ROWS, LANES), F32),
                vmem((ROWS, LANES), F32),
                vmem((ROWS, LANES), F32),
                vmem((ROWS, LANES), F32),
                vmem((ROWS, LANES), F32),
                vmem((2, ROWS, LANES), F32),
                vmem((2, ROWS, LANES), F32),
                vmem((ROWS, ROWS), BF16),
                vmem((ROWS, ROWS), BF16),
                pltpu.SemaphoreType.DMA((2 * CHUNKS + 1,)),
                pltpu.SemaphoreType.DMA((copies,)),
                pltpu.SemaphoreType.DMA((copies,)),
                *(vmem(shape, F32) for shape in shapes),
            ],
            compiler_params=pltpu.CompilerParams(
                collective_id=0, has_side_effects=True, vmem_limit_bytes=54_550_000
            ),
        )(data, maps)
        return pl.pallas_call(
            finish,
            name="srm_maps",
            out_shape=(
                jax.ShapeDtypeStruct((trs, k), F32),
                jax.ShapeDtypeStruct((1, k, vectors), BF16),
            ),
            in_specs=[held] * 5,
            out_specs=[hbm] * 2,
            scratch_shapes=[vmem((k, vectors), BF16), pltpu.SemaphoreType.DMA((8,))],
            compiler_params=pltpu.CompilerParams(vmem_limit_bytes=16 << 20),
        )(*parts)

    return jax.shard_map(
        shards,
        mesh=grid,
        in_specs=(P("subj", None, vox), P("subj", None, vox)),
        out_specs=(P(), P("subj", None, vox)),
        check_vma=False,
    )
```

```python
import functools

import jax
import jax.numpy as jnp
from jax import lax
from jax.experimental import pallas as pl
from jax.experimental.pallas import tpu as pltpu
from jax.sharding import Mesh
from jax.sharding import PartitionSpec as P

NS_STEPS = 5
LANES = 128
ROWS = 512
CHUNKS = 4
LAG = 4
HALF = ROWS // 2
SUMS = (
    ("r", 0, HALF, "subj", ("x", "y")),
    ("r", HALF, HALF, "y", ("x", "subj")),
)
MESH = pl.DeviceIdType.MESH
F32, BF16 = jnp.float32, jnp.bfloat16


def dot(a, b):
    return jnp.dot(a, b, preferred_element_type=F32)


def dot_nt(a, b):
    return lax.dot_general(a, b, (((1,), (1,)), ((), ())), preferred_element_type=F32)


def split(a):
    high = a.astype(BF16)
    return high, (a - high.astype(F32)).astype(BF16)


def dot3(a, b):
    ah, al = a
    bh, bl = b
    return dot(ah, bh) + (dot(ah, bl) + dot(al, bh))


def kernel(
    sizes,
    subjects,
    data_hbm,
    maps_hbm,
    p_hi,
    p_lo,
    a_hi,
    a_lo,
    resp,
    d,
    end,
    w,
    part_r,
    part_c,
    pair_r,
    pair_c,
    sum_r,
    sum_c,
    full_r,
    full_c,
    gram_hi,
    gram_lo,
    local_sem,
    send_sem,
    recv_sem,
    *buffers,
):
    nz, ny, nx = sizes
    trs = data_hbm.shape[1]
    me = {name: lax.axis_index(name) for name in ("subj", "y", "x", "core")}
    size = {"subj": nz, "y": ny, "x": nx, "core": 2}
    core = me["core"]
    other = 1 - core

    edge = trs // 16 * 16
    chunk = d.shape[1] // CHUNKS
    load_end = pltpu.make_async_copy(
        data_hbm.at[0, pl.ds(edge, trs - edge)], end, local_sem.at[2 * CHUNKS]
    )
    load_end.start()
    loads = []
    for i in range(CHUNKS):
        part = pl.ds(i * chunk, chunk)
        load_d = pltpu.make_async_copy(
            data_hbm.at[0, pl.ds(0, edge), part], d.at[pl.ds(0, edge), part], local_sem.at[2 * i]
        )
        load_w = pltpu.make_async_copy(
            maps_hbm.at[0, :, part], w.at[:, part], local_sem.at[2 * i + 1]
        )
        load_d.start()
        load_w.start()
        loads.append((part, load_d, load_w))

    barrier = pltpu.get_barrier_semaphore()
    partners = sorted(
        ((axis, s) for axis, n in size.items() for s in range(1, n)),
        key=lambda p: -min(p[1], size[p[0]] - p[1]),
    )
    for axis, s in partners:
        pl.semaphore_signal(
            barrier,
            inc=1,
            device_id={axis: lax.rem(me[axis] + s, size[axis])},
            device_id_type=MESH,
        )

    pending = []

    def send(src, dst, axis, s, arrived):
        k = len(pending)
        copy = pltpu.make_async_remote_copy(
            src_ref=src,
            dst_ref=dst,
            send_sem=send_sem.at[k],
            recv_sem=recv_sem.at[k],
            device_id={axis: lax.rem(me[axis] + s, size[axis])},
            device_id_type=MESH,
        )
        copy.start()
        pending.append(copy)
        back = pltpu.make_async_remote_copy(
            src_ref=src,
            dst_ref=arrived,
            send_sem=send_sem.at[k],
            recv_sem=recv_sem.at[k],
            device_id={axis: lax.rem(me[axis] + s, size[axis])},
            device_id_type=MESH,
        )
        return back.wait_recv

    def nosend(*a):
        return lambda: None

    def near_first(n):
        return sorted(range(1, n), key=lambda s: min(s, n - s))

    def far_first(n):
        return near_first(n)[::-1]

    def ahead(axis, s):
        return lax.rem(me[axis] + s, size[axis])

    def behind(axis, s):
        return lax.rem(me[axis] + (size[axis] - s), size[axis])

    def rows(start, count):
        return pl.ds(pl.multiple_of(start, 8), count)

    zeros = jnp.zeros((LANES, LANES), F32)
    for slot in range(4):
        part_c[1, pl.ds(slot * LANES, LANES)] = zeros
    load_end.wait()
    d[pl.ds(edge, ROWS - edge), :] = jnp.concatenate(
        [end[...], jnp.zeros((ROWS - trs, d.shape[1]), BF16)], axis=0
    )
    partial = None
    for part, load_d, load_w in loads:
        load_d.wait()
        load_w.wait()
        term = dot_nt(d[:, part], w[:, part])
        partial = term if partial is None else partial + term
    part_r[0] = partial[:, :LANES]
    part_r[1] = partial[:, LANES:]
    pl.semaphore_wait(barrier, len(partners))
    got_pair_r = send(part_r.at[other], pair_r, "core", 1, pair_r)

    row = lax.broadcasted_iota(jnp.int32, (LANES, LANES), 0)
    col = lax.broadcasted_iota(jnp.int32, (LANES, LANES), 1)
    top = dot_nt(d[pl.ds(0, HALF), :], d[pl.ds(0, HALF), :])
    c00, c10, c11 = top[:LANES, :LANES], top[LANES:, :LANES], top[LANES:, LANES:]
    part_c[0, pl.ds(0, LANES)] = c10
    part_c[0, pl.ds(3 * LANES, LANES)] = jnp.where(row >= col, c00, c11)
    low = dot_nt(d[pl.ds(HALF, HALF), :], d[...])
    part_c[0, pl.ds(LANES, LANES)] = low[:LANES, :LANES]
    part_c[0, pl.ds(2 * LANES, LANES)] = low[:LANES, LANES : 2 * LANES]
    c22 = low[:LANES, 2 * LANES : 3 * LANES]
    c33 = low[LANES:, 3 * LANES :]
    last = 72
    for slot in range(3):
        part_c[1, pl.ds(slot * LANES, last)] = low[
            LANES : LANES + last, slot * LANES : (slot + 1) * LANES
        ]
    part_c[1, pl.ds(3 * LANES, LANES)] = jnp.where(row >= col, c22, c33)
    on_diagonal = row == col
    for slot, block in ((0, c11), (1, c33)):
        diagonal = jnp.sum(jnp.where(on_diagonal, block, 0.0), axis=0, keepdims=True)
        part_c[1, pl.ds(slot * LANES + 80, 8)] = jnp.broadcast_to(diagonal, (8, LANES))
    got_pair_c = send(part_c.at[other], pair_c, "core", 1, pair_c)

    got_other = {"r": [], "c": []}

    def summed(name, source, full, factor, start, count, axis, others, buffers):
        n = size[axis]
        block = count // n
        arrived, *swaps = buffers
        got = {}

        def place(at):
            return rows(start + at * block, block)

        for s in far_first(n):
            slot = arrived.at[s - 1]
            got[s] = send(source.at[place(ahead(axis, s))], slot, axis, s, slot)
            yield
        total = source[place(me[axis])]
        for s in far_first(n):
            got[s]()
            total = total + arrived[s - 1]
        for across, swap in zip(others, swaps):
            m = size[across]
            mine = swap.at[me[across]]
            mine[...] = total
            for s in far_first(m):
                got[s] = send(mine, mine, across, s, swap.at[behind(across, s)])
            yield
            for s in far_first(m):
                got[s]()
            total = swap[0]
            for i in range(1, m):
                total = total + swap[i]
        mine = full.at[core, place(me[axis])]
        mine[...] = total * factor
        for s in far_first(n):
            got[s] = send(mine, mine, axis, s, full.at[core, place(behind(axis, s))])
        yield
        for s in far_first(n):
            got[s]()
        here = rows(start, count)
        mine = full.at[core, here]
        got_other[name].append(send(mine, mine, "core", 1, full.at[other, here]))
        yield

    block_x = ROWS // nx
    fine = block_x // ny

    def gram_sum(buffers):
        c1, c2_sum, c2 = buffers
        got = {}

        def place(x):
            return rows(x * block_x, block_x)

        def fine_place(x, y):
            return rows(x * block_x + y * fine, fine)

        for s in far_first(nx):
            slot = c1.at[s - 1]
            got[s] = send(sum_c.at[place(ahead("x", s))], slot, "x", s, slot)
        yield
        total = sum_c[place(me["x"])]
        for s in near_first(nx):
            got[s]()
            total = total + c1[s - 1]
        c2_sum[...] = total
        for s in far_first(ny):
            slot = c2.at[s - 1]
            got[s] = send(c2_sum.at[rows(ahead("y", s) * fine, fine)], slot, "y", s, slot)
        yield
        total = c2_sum[rows(me["y"] * fine, fine)]
        for s in far_first(ny):
            got[s]()
            total = total + c2[s - 1]
        mine = full_c.at[core, fine_place(me["x"], me["y"])]
        mine[...] = total
        for s in far_first(ny):
            there = full_c.at[core, fine_place(me["x"], behind("y", s))]
            got[s] = send(mine, mine, "y", s, there)
        yield
        for s in far_first(ny):
            got[s]()
        mine = full_c.at[core, place(me["x"])]
        for s in far_first(nx):
            got[s] = send(mine, mine, "x", s, full_c.at[core, place(behind("x", s))])
        yield
        for s in near_first(nx):
            got[s]()
        mine = full_c.at[core]
        got_other["c"].append(send(mine, mine, "core", 1, full_c.at[other]))
        yield

    marks = []
    drained = 0

    def drain(upto):
        nonlocal drained
        for copy in pending[drained:upto]:
            copy.wait_send()
        drained = max(drained, upto)

    def step(*chains):
        for chain in chains:
            next(chain)
        marks.append(len(pending))
        if len(marks) > LAG:
            drain(marks[-1 - LAG])

    rest = iter(buffers)
    chains = []
    for name, start, count, axis, others in SUMS:
        source, full, factor = (
            (sum_r, full_r, 1.0 / subjects) if name == "r" else (sum_c, full_c, 1.0)
        )
        own = [next(rest) for _ in range(1 + len(others))]
        chains.append(summed(name, source, full, factor, start, count, axis, others, own))
    r0, r1 = chains
    c0 = gram_sum(list(rest))
    got_pair_r()
    sum_r[...] = part_r[core] + pair_r[...]
    for _ in range(nz - 2):
        next(r0)
        next(r1)
    step(r0, r1)
    got_pair_c()
    sum_c[...] = part_c[core] + pair_c[...]
    step(c0)
    step(c0)
    step(r0, r1)
    step(r0, r1)
    step(c0)
    step(r0, r1)
    step(c0)
    step(r0, r1)
    step(c0)
    for wait in got_other["c"]:
        wait()

    def put(i, j, block):
        high, low_part = split(block)
        gram_hi[pl.ds(i * LANES, LANES), pl.ds(j * LANES, LANES)] = high
        gram_lo[pl.ds(i * LANES, LANES), pl.ds(j * LANES, LANES)] = low_part

    def put_both(i, j, block):
        put(i, j, block)
        put(j, i, block.T)

    put_both(1, 0, full_c[0, pl.ds(0, LANES)])
    put_both(2, 0, full_c[0, pl.ds(LANES, LANES)])
    put_both(2, 1, full_c[0, pl.ds(2 * LANES, LANES)])
    for slot in range(3):
        block = full_c[1, pl.ds(slot * LANES, LANES)]
        put_both(3, slot, jnp.where(row < last, block, 0.0))
    for half, i, j in ((0, 0, 1), (1, 2, 3)):
        packed = full_c[half, pl.ds(3 * LANES, LANES)]
        turned = packed.T
        diagonal = full_c[1, pl.ds(half * LANES + 80, 8)][:1]
        put(i, i, jnp.where(row >= col, packed, turned))
        block = jnp.where(row < col, packed, turned)
        put(j, j, jnp.where(on_diagonal, jnp.broadcast_to(diagonal, block.shape), block))

    for wait in got_other["r"]:
        wait()

    response = jnp.concatenate([full_r[0], full_r[1]], axis=1)
    resp[...] = response[:trs]
    shared = response.astype(BF16)
    shared_t = shared.T
    t_hi, t_lo = split(dot(shared_t, gram_hi[...]) + dot(shared_t, gram_lo[...]))
    gram = dot(t_hi, shared) + dot(t_lo, shared)
    k = gram.shape[0]

    scale = jnp.sqrt(jnp.sum(gram * gram, keepdims=True) + 1e-06)
    estimate = gram / scale
    unit = lax.broadcasted_iota(jnp.int32, (k, k), 0) == lax.broadcasted_iota(
        jnp.int32, (k, k), 1
    )
    one = jnp.where(unit, 1.0, 0.0).astype(F32)
    split_x = split(estimate)
    product = None
    for step_pair in range(NS_STEPS // 2):
        x = estimate
        xs = split_x
        x2 = dot3(xs, xs)
        quartic = dot3(split(x2), split(0.0625 * x2 - 0.5625 * x))
        factor = split(2.25 * one - 2.4375 * x + 1.6875 * x2 + quartic)
        if product is None:
            a_hi[...], a_lo[...] = split(dot(shared_t, d[...]))
            xq = dot3(xs, factor)
            product = factor
        else:
            stacked = tuple(jnp.concatenate(pair, axis=0) for pair in zip(xs, product))
            both = dot3(stacked, factor)
            xq, product = both[:k], split(both[k:])
        estimate = dot3(split(xq), factor)
        split_x = split(estimate)
    if NS_STEPS % 2:
        inverse = dot3(split(1.5 * one - 0.5 * estimate), product)
    else:
        inverse = product[0].astype(F32) + product[1].astype(F32)
    p_hi[...], p_lo[...] = split(inverse * (1.0 / jnp.sqrt(scale)))
    drain(len(pending))


def finish(p_hi, p_lo, a_hi, a_lo, resp, resp_hbm, new_hbm, new, sem):
    store_r = pltpu.make_async_copy(resp, resp_hbm, sem.at[0])
    store_r.start()
    stores = []
    width = 256
    for i in range(new.shape[1] // width):
        part = pl.ds(i * width, width)
        out = dot3((p_hi[...], p_lo[...]), (a_hi[:, part], a_lo[:, part]))
        new[:, part] = out.astype(BF16)
        store = pltpu.make_async_copy(new.at[:, part], new_hbm.at[0, :, part], sem.at[1 + i])
        store.start()
        stores.append(store)
    for store in stores:
        store.wait()
    store_r.wait()


def solution(mesh):
    nz, ny, nx = mesh.shape["subj"], 8, 4
    names = ("subj", "y", "x", "core")
    return build(Mesh(mesh.devices.reshape(nz, ny, nx, 2), names))


def build(grid):
    vox = ("y", "x", "core")
    nz, ny, nx = (grid.shape[name] for name in ("subj", "y", "x"))
    size = {"subj": nz, "y": ny, "x": nx}
    shapes = []
    copies = 2
    for _, _, count, axis, others in SUMS:
        block = count // size[axis]
        shapes.append((size[axis] - 1, block, LANES))
        shapes += [(size[across], block, LANES) for across in others]
        copies += 2 * size[axis] - 1 + sum(size[across] - 1 for across in others)
    block_x = ROWS // nx
    shapes += [(nx - 1, block_x, LANES), (block_x, LANES), (ny - 1, block_x // ny, LANES)]
    copies += 2 * (nx + ny)

    def shards(data, maps):
        _, trs, vectors = data.shape
        k = maps.shape[1]
        subjects = nz * data.shape[0]
        vmem = pltpu.VMEM
        held = pl.BlockSpec(memory_space=pltpu.VMEM)
        hbm = pl.BlockSpec(memory_space=pltpu.HBM)
        parts = pl.pallas_call(
            functools.partial(kernel, (nz, ny, nx), subjects),
            name="srm_step",
            out_shape=(
                jax.ShapeDtypeStruct((k, k), BF16),
                jax.ShapeDtypeStruct((k, k), BF16),
                jax.ShapeDtypeStruct((k, vectors), BF16),
                jax.ShapeDtypeStruct((k, vectors), BF16),
                jax.ShapeDtypeStruct((trs, k), F32),
            ),
            in_specs=[hbm] * 2,
            out_specs=[held] * 5,
            scratch_shapes=[
                vmem((ROWS, vectors), BF16),
                vmem((trs % 16, vectors), BF16),
                vmem((k, vectors), BF16),
                vmem((2, ROWS, LANES), F32),
                vmem((2, ROWS, LANES), F32),
                vmem((ROWS, LANES), F32),
                vmem((ROWS, LANES), F32),
                vmem((ROWS, LANES), F32),
                vmem((ROWS, LANES), F32),
                vmem((2, ROWS, LANES), F32),
                vmem((2, ROWS, LANES), F32),
                vmem((ROWS, ROWS), BF16),
                vmem((ROWS, ROWS), BF16),
                pltpu.SemaphoreType.DMA((2 * CHUNKS + 1,)),
                pltpu.SemaphoreType.DMA((copies,)),
                pltpu.SemaphoreType.DMA((copies,)),
                *(vmem(shape, F32) for shape in shapes),
            ],
            compiler_params=pltpu.CompilerParams(
                collective_id=0, has_side_effects=True, vmem_limit_bytes=54_550_000
            ),
        )(data, maps)
        return pl.pallas_call(
            finish,
            name="srm_maps",
            out_shape=(
                jax.ShapeDtypeStruct((trs, k), F32),
                jax.ShapeDtypeStruct((1, k, vectors), BF16),
            ),
            in_specs=[held] * 5,
            out_specs=[hbm] * 2,
            scratch_shapes=[vmem((k, vectors), BF16), pltpu.SemaphoreType.DMA((8,))],
            compiler_params=pltpu.CompilerParams(vmem_limit_bytes=16 << 20),
        )(*parts)

    return jax.shard_map(
        shards,
        mesh=grid,
        in_specs=(P("subj", None, vox), P("subj", None, vox)),
        out_specs=(P(), P("subj", None, vox)),
        check_vma=False,
    )
```
